32 devices in a mesh: dp: 16 (over z, y, x), tensor: 2 (over core).
Axes of the slice: x: 2, y: 2, z: 4, core: 2. Of those that a mesh axis runs over, the one named last changes fastest.
Arguments:
- media: bfloat16 [64, 576, 1024], P('dp'), may hold values from -6 to 6
- buckets: int32 [64], P('dp'), may hold values 0 or 1
- latents: bfloat16 [64, 64, 1024], P('dp'), may hold values from -6 to 6
- cotangent: bfloat16 [64, 64, 1024], P('dp'), may hold values from -6 to 6
- query_weight: bfloat16 [1024, 512], P(None, 'tensor'), may hold values from -0.375 to 0.375
- key_weight: bfloat16 [1024, 512], P(None, 'tensor'), may hold values from -0.1875 to 0.1875
- value_weight: bfloat16 [1024, 512], P(None, 'tensor'), may hold values from -0.1875 to 0.1875
- output_weight: bfloat16 [512, 1024], P('tensor'), may hold values from -2 to 2
- up_weight: bfloat16 [1024, 4096], P(None, 'tensor'), may hold values from -0.1875 to 0.1875
- down_weight: bfloat16 [4096, 1024], P('tensor'), may hold values from -0.125 to 0.125
- media_gain: float32 [1024], replicated, may hold values from 0.1 to 1.9
- media_bias: float32 [1024], replicated, may hold values from -1.5 to 1.5
- latent_gain: float32 [1024], replicated, may hold values from 0.1 to 1.9
- latent_bias: float32 [1024], replicated, may hold values from -1.5 to 1.5
- feed_gain: float32 [1024], replicated, may hold values from 0.1 to 1.9
- feed_bias: float32 [1024], replicated, may hold values from -1.5 to 1.5
Outputs:
- latents_out: bfloat16 [64, 64, 1024], P('dp')
- grad_media: bfloat16 [64, 576, 1024], P('dp')
- grad_latents: bfloat16 [64, 64, 1024], P('dp')
- grad_query_weight: float32 [1024, 512], P('dp', 'tensor')
- grad_key_weight: float32 [1024, 512], P('dp', 'tensor')
- grad_value_weight: float32 [1024, 512], P('dp', 'tensor')
- grad_output_weight: float32 [512, 1024], P('tensor', 'dp')
- grad_up_weight: float32 [1024, 4096], P('dp', 'tensor')
- grad_down_weight: float32 [4096, 1024], P('tensor', 'dp')
- grad_media_gain: float32 [1024], P('dp')
- grad_media_bias: float32 [1024], P('dp')
- grad_latent_gain: float32 [1024], P('dp')
- grad_latent_bias: float32 [1024], P('dp')
- grad_feed_gain: float32 [1024], P('dp')
- grad_feed_bias: float32 [1024], P('dp')
The draws below stay inside these ranges and needn't reach their ends.
Inputs may be any that keep to these rules, and one draw needn't show every extreme that they name: `buckets`: bucket 1 marks an image with 576 patches, 0 one with 256; patch slots past an image's count are padding.
All inputs are finite; a program needn't handle non-finite values. No bound on the sum of `buckets` on one device may be relied on, other than what follows from the above.
Results may differ from the reference program's by a relative error of at most 0.014.
The reference program's roundings to bfloat16 on the way count: a program that leaves them out, or rounds other values in their place, can miss the bound.
Values sent between devices are 32-bit elements; how exact they have to be, the bound alone decides.
No kernel may reach another device: no remote copies, remote signals or barrier semaphores. Data moves between devices by JAX's collectives and lax.ppermute only.
A program may use at most 192 MiB of HBM per device.

```python
import jax
import jax.numpy as jnp
from jax import lax

D = 1024
HEADS = 8
HEAD = 64
FF = 4096
LAT = 64
PATCH = 576
SHORT = 256
INNER = 512
IMAGES = 64


def touch_ends(entries, own_key, least, largest):
    dims = entries.shape
    spot = [jax.random.randint(jax.random.fold_in(own_key, axis), (), 0, dims[axis]) for axis in range(len(dims))]
    entries = entries.at[tuple(spot)].set(least)
    longest = dims.index(max(dims))
    spot[longest] = (spot[longest] + 1) % dims[longest]
    return entries.at[tuple(spot)].set(largest)


def block_levels(stream_key, shape, cuts, low, top_value):
    def one(axis_at, parts):
        heights = jax.random.uniform(jax.random.fold_in(jax.random.fold_in(stream_key, 6), axis_at), (parts,), jnp.float32, low / len(cuts), top_value / len(cuts))
        return jnp.repeat(jnp.exp(heights), shape[axis_at] // parts).reshape((-1,) + (1,) * (len(shape) - axis_at - 1))

    level = one(*cuts[0])
    for cut in cuts[1:]:
        level = level * one(*cut)
    return level


def scatter_about(stream_key, dims, deviation, most, cuts=(), kind=jnp.bfloat16):
    array = deviation * jax.random.normal(stream_key, dims, jnp.float32)
    if cuts:
        array = array * block_levels(stream_key, dims, cuts, -0.22, 0.18)
    return jnp.clip(array, -most, most).astype(kind)


def setup_inputs(seed: int = 0) -> dict:
    streams_of = jax.random.split(jax.random.key(seed), 17)
    return {
        "media": scatter_about(streams_of[0], (IMAGES, PATCH, D), 1.0, 6.0, ((0, 16),)),
        "buckets": touch_ends((jax.random.randint(streams_of[1], (IMAGES,), 0, 7) < 4).astype(jnp.int32), jax.random.fold_in(streams_of[1], 1), 0, 1),
        "latents": scatter_about(streams_of[2], (IMAGES, LAT, D), 1.0, 6.0, ((0, 16),)),
        "cotangent": scatter_about(streams_of[3], (IMAGES, LAT, D), 1.0, 6.0, ((0, 16),)),
        "query_weight": scatter_about(streams_of[4], (D, INNER), (D // 4) ** -0.5, 0.375, ((1, 2),)),
        "key_weight": scatter_about(streams_of[5], (D, INNER), D ** -0.5, 0.1875, ((1, 2),)),
        "value_weight": scatter_about(streams_of[6], (D, INNER), D ** -0.5, 0.1875, ((1, 2),)),
        "output_weight": scatter_about(streams_of[7], (INNER, D), (INNER // 64) ** -0.5, 2.0, ((0, 2),)),
        "up_weight": scatter_about(streams_of[8], (D, FF), D ** -0.5, 0.1875, ((1, 2),)),
        "down_weight": scatter_about(streams_of[9], (FF, D), (FF // 2) ** -0.5, 0.125, ((0, 2),)),
        "media_gain": jnp.clip(1.0 + 0.18 * jax.random.normal(streams_of[10], (D,), jnp.float32), 0.1, 1.9),
        "media_bias": scatter_about(streams_of[11], (D,), 0.3, 1.5, (), jnp.float32),
        "latent_gain": jnp.clip(1.0 + 0.18 * jax.random.normal(streams_of[12], (D,), jnp.float32), 0.1, 1.9),
        "latent_bias": scatter_about(streams_of[13], (D,), 0.3, 1.5, (), jnp.float32),
        "feed_gain": jnp.clip(1.0 + 0.18 * jax.random.normal(streams_of[14], (D,), jnp.float32), 0.1, 1.9),
        "feed_bias": scatter_about(streams_of[15], (D,), 0.3, 1.5, (), jnp.float32),
    }


@jax.custom_vjp
def low(v):
    return lax.optimization_barrier(v.astype(jnp.bfloat16)).astype(jnp.float32)

@jax.custom_vjp
def low_back(v):
    return v

def low_keep(v):
    return (low(v), None)

def low_pass(kept, grad):
    return (grad,)

def back_keep(v):
    return (v, None)

def back_low(kept, grad):
    return (low(grad),)
low.defvjp(low_keep, low_pass)
low_back.defvjp(back_keep, back_low)
HIGHEST = lax.Precision.HIGHEST

def layer_norm(values, gain, offset):
    center = values - lax.optimization_barrier(jnp.mean(values, -1, keepdims=True))
    return center * lax.rsqrt(lax.optimization_barrier(jnp.mean(center * center, -1, keepdims=True)) + 1e-05) * gain + offset

def matmul(left, right):
    return jnp.dot(left, right, precision=HIGHEST)

def reference(media, buckets, latents, cotangent, query_weight, key_weight, value_weight, output_weight, up_weight, down_weight, media_gain, media_bias, latent_gain, latent_bias, feed_gain, feed_bias):
    counts = SHORT + (PATCH - SHORT) * buckets
    position = jnp.arange(PATCH + LAT, dtype=jnp.int32)
    usable = (position[None, :] < counts[:, None]) | (position[None, :] >= PATCH)
    factor = HEAD ** (-0.5)

    def forward(media_all, latent_all, weight_q, weight_k, weight_v, weight_o, weight_up, weight_down, gain_m, bias_m, gain_l, bias_l, gain_f, bias_f):

        def single(items):
            media_one, latent_one, usable_one = items
            media_norm = low(layer_norm(media_one, gain_m, bias_m))
            latent_norm = low(layer_norm(latent_one, gain_l, bias_l))
            kv_input = jnp.concatenate([media_norm, latent_norm], 0)
            queries = low_back(low(matmul(latent_norm, weight_q))).reshape(LAT, HEADS, HEAD)
            keys = low_back(low(matmul(kv_input, weight_k))).reshape(PATCH + LAT, HEADS, HEAD)
            values = low_back(low(matmul(kv_input, weight_v))).reshape(PATCH + LAT, HEADS, HEAD)
            scores = low_back(jnp.einsum('rhc,khc->hrk', queries, keys, precision=HIGHEST) * factor)
            scores = jnp.where(usable_one[None, None, :], scores, -1e+30)
            probs = low(jax.nn.softmax(scores, axis=-1))
            attended = jnp.einsum('hrk,khc->rhc', probs, values, precision=HIGHEST).reshape(LAT, INNER)
            attended = low_back(low(attended))
            middle = latent_one + low_back(matmul(attended, weight_o))
            feed_norm = low(layer_norm(middle, gain_f, bias_f))
            hidden = low(jax.nn.gelu(low_back(matmul(feed_norm, weight_up)), approximate=False))
            return middle + low_back(matmul(hidden, weight_down))
        return lax.map(jax.checkpoint(single), (media_all, latent_all, usable))
    inputs = (media.astype(jnp.float32), latents.astype(jnp.float32), query_weight.astype(jnp.float32), key_weight.astype(jnp.float32), value_weight.astype(jnp.float32), output_weight.astype(jnp.float32), up_weight.astype(jnp.float32), down_weight.astype(jnp.float32), media_gain, media_bias, latent_gain, latent_bias, feed_gain, feed_bias)
    result, backward = jax.vjp(forward, *inputs)
    grads = backward(cotangent.astype(jnp.float32))
    return (result.astype(jnp.bfloat16), grads[0].astype(jnp.bfloat16), grads[1].astype(jnp.bfloat16), grads[2], grads[3], grads[4], grads[5], grads[6], grads[7], grads[8], grads[9], grads[10], grads[11], grads[12], grads[13])
```

```python
import jax
import jax.numpy as jnp
from jax import lax
from jax.experimental import pallas as pl
from jax.sharding import PartitionSpec as P

HEAD = 64
PATCH = 576
SHORT = 256
GROUP = 4
EPSILON = 1e-05
SINGLE = jnp.float32
HALF = jnp.bfloat16


def layer_norm(values, gain, offset):
    center = values - jnp.mean(values, -1, keepdims=True)
    inverse = lax.rsqrt(jnp.mean(center * center, -1, keepdims=True) + EPSILON)
    normed = center * inverse
    return (normed * gain + offset, normed, inverse)


def norm_back(upstream, normed, inverse, gain):
    scaled = upstream * gain
    result = inverse * (
        scaled
        - jnp.mean(scaled, -1, keepdims=True)
        - normed * jnp.mean(scaled * normed, -1, keepdims=True)
    )
    return (result, jnp.sum(upstream * normed, axis=(0, 1)), jnp.sum(upstream, axis=(0, 1)))


def exact_gelu(values):
    return jax.nn.gelu(values, approximate=False)


def narrow_body(wide_ref, low_ref):
    low_ref[...] = wide_ref[...].astype(HALF)


def narrow(array):
    count, width = array.shape
    block = 256 if count % 256 == 0 else count
    spec = pl.BlockSpec((block, width), lambda at: (at, 0))
    return pl.pallas_call(
        narrow_body,
        grid=(count // block,),
        in_specs=[spec],
        out_specs=spec,
        out_shape=jax.ShapeDtypeStruct(array.shape, HALF),
        cost_estimate=pl.CostEstimate(
            flops=array.size, bytes_accessed=6 * array.size, transcendentals=0
        ),
        name="narrow",
    )(array)


def pick(array, index, axis):
    return lax.dynamic_index_in_dim(array, index, axis, keepdims=False)


class Links:
    def __init__(self, devices):
        self.devices = devices
        self.bits = devices.bit_length() - 1
        self.row = lax.axis_index("dp")
        self.core = lax.axis_index("tensor")

    def swap(self, array):
        return lax.ppermute(array, "tensor", [(0, 1), (1, 0)])

    def send(self, array, step_zero, step_one):
        pairs = []
        for row in range(self.devices):
            pairs.append((2 * row, 2 * (row ^ step_zero)))
            pairs.append((2 * row + 1, 2 * (row ^ step_one) + 1))
        return lax.ppermute(array, ("dp", "tensor"), pairs)

    def bit(self, which):
        return (self.row >> which) & 1

    def halve(self, blocks, low, high):
        own = self.core == 0
        at = low
        while at < high:
            count = blocks.shape[0]
            rest = blocks.shape[1:]
            if at + 1 < high:
                grid = blocks.reshape((count // 4, 2, 2) + rest)
                first, second = self.bit(at), self.bit(at + 1)
                out = jnp.where(own, pick(grid, 1 - first, 2), pick(grid, 1 - second, 1))
                keep = jnp.where(own, pick(grid, first, 2), pick(grid, second, 1))
                part = keep + self.send(out, 1 << at, 2 << at)
                other = jnp.where(own, second, first)
                blocks = pick(part, other, 1) + self.send(
                    pick(part, 1 - other, 1), 2 << at, 1 << at
                )
                at += 2
            else:
                grid = blocks.reshape((count // 2, 2) + rest)
                mine = self.bit(at)
                blocks = pick(grid, mine, 1) + self.send(pick(grid, 1 - mine, 1), 1 << at, 1 << at)
                at += 1
        return blocks[0]

    def gather(self, rows):
        half = rows.shape[0] // 2
        own = lax.dynamic_slice_in_dim(rows, self.core * half, half, 0)
        near = self.send(own, 1, 2)
        pair = jnp.concatenate([own, near], 0)
        far = self.send(pair, 2, 1)
        mine = jnp.concatenate([pair, far], 0)
        return jnp.concatenate([mine, self.swap(mine)], 0)

    def spread(self, blocks):
        member = self.row % GROUP
        got = [pick(blocks, member, 0)]
        for step in range(1, GROUP):
            got.append(self.send(pick(blocks, member ^ step, 0), step, step))
        stack = jnp.stack(got)
        return [pick(stack, member ^ place, 0) for place in range(GROUP)]


def dot(form, left, right):
    return jnp.einsum(form, left, right, preferred_element_type=SINGLE)


def local(
    media,
    buckets,
    latents,
    cotangent,
    query_weight,
    key_weight,
    value_weight,
    output_weight,
    up_weight,
    down_weight,
    media_gain,
    media_bias,
    latent_gain,
    latent_bias,
    feed_gain,
    feed_bias,
    devices,
):
    links = Links(devices)
    images, patches, width = media.shape
    latent_rows = latents.shape[1]
    rows_here = images * latent_rows
    keys_all = patches + latent_rows
    inner_here = query_weight.shape[1]
    heads_here = inner_here // HEAD
    hidden_here = up_weight.shape[1]
    factor = HEAD ** (-0.5)
    cot_rows = cotangent.reshape(rows_here, width)
    cot_all = narrow(links.gather(cot_rows.astype(SINGLE)))
    weights_other = narrow(
        links.swap(jnp.concatenate([query_weight, key_weight, value_weight], 1).astype(SINGLE))
    )
    media_norm, media_hat, media_inv = layer_norm(media.astype(SINGLE), media_gain, media_bias)
    latent_in = latents.astype(SINGLE)
    latent_norm, latent_hat, latent_inv = layer_norm(latent_in, latent_gain, latent_bias)
    kv_input = jnp.concatenate([media_norm.astype(HALF), latent_norm.astype(HALF)], axis=1)
    query_input = kv_input[:, patches:]
    queries = dot("ird,de->ire", query_input, query_weight).astype(HALF)
    keys = dot("ikd,de->ike", kv_input, key_weight).astype(HALF)
    values = dot("ikd,de->ike", kv_input, value_weight).astype(HALF)
    query_heads = queries.reshape(images, latent_rows, heads_here, HEAD)
    key_heads = keys.reshape(images, keys_all, heads_here, HEAD)
    value_heads = values.reshape(images, keys_all, heads_here, HEAD)
    counts = SHORT + (PATCH - SHORT) * buckets
    position = lax.broadcasted_iota(jnp.int32, (images, keys_all), 1)
    usable = (position < counts[:, None]) | (position >= patches)
    scores = dot("irhc,ikhc->ihrk", query_heads, key_heads) * factor
    scores = jnp.where(usable[:, None, None, :], scores, -1e30)
    shifted = jnp.exp(scores - jnp.max(scores, -1, keepdims=True))
    probs = shifted / jnp.sum(shifted, -1, keepdims=True)
    probs_low = probs.astype(HALF)
    attended = dot("ihrk,ikhc->irhc", probs_low, value_heads)
    attended = attended.reshape(images, latent_rows, inner_here).astype(HALF)
    branch = dot("ire,ed->ird", attended, output_weight)
    middle = latent_in + (branch + links.swap(branch))
    feed_norm, feed_hat, feed_inv = layer_norm(middle, feed_gain, feed_bias)
    feed_low = feed_norm.astype(HALF)
    feed_all = narrow(links.gather(feed_low.astype(SINGLE).reshape(rows_here, width)))
    hidden_pre = dot("ird,df->irf", feed_low, up_weight)
    hidden_low = exact_gelu(hidden_pre).astype(HALF)
    grad_hidden = dot("ird,fd->irf", cotangent, down_weight)
    unused_value, gelu_back = jax.vjp(exact_gelu, hidden_pre)
    grad_pre = gelu_back(grad_hidden)[0].astype(HALF)
    feed_part = dot("irf,df->ird", grad_pre, up_weight)
    grad_feed = feed_part + links.swap(feed_part)
    feed_out = dot("irf,fd->ird", hidden_low, down_weight)
    result = (middle + (feed_out + links.swap(feed_out))).astype(HALF)
    grad_middle_norm, grad_feed_gain, grad_feed_bias = norm_back(
        grad_feed, feed_hat, feed_inv, feed_gain
    )
    grad_middle = cotangent.astype(SINGLE) + grad_middle_norm
    grad_branch = grad_middle.astype(HALF)

    member = links.row % GROUP
    piece = hidden_here // GROUP
    up_piece = lax.dynamic_slice_in_dim(up_weight, member * piece, piece, 1)
    down_piece = lax.dynamic_slice_in_dim(down_weight, member * piece, piece, 0)
    pre_all = dot("rd,df->rf", feed_all, up_piece)
    hidden_all = exact_gelu(pre_all).astype(HALF)
    back_all = dot("rd,fd->rf", cot_all, down_piece)
    grad_pre_all = jax.vjp(exact_gelu, pre_all)[1](back_all)[0].astype(HALF)
    grad_up = dot("rd,rf->df", feed_all, grad_pre_all)
    grad_down = dot("rd,rf->df", cot_all, hidden_all)
    wide = jnp.concatenate([grad_up, grad_down], 1).reshape(devices // GROUP, -1, 2 * piece)
    wide = links.halve(wide, 2, links.bits)
    share = wide.shape[0] // GROUP
    wide = links.spread(wide.reshape(GROUP, share, 2 * piece))
    grad_up = jnp.concatenate([block[:, :piece] for block in wide], 1)
    grad_down = jnp.concatenate([block[:, piece:] for block in wide], 1).T

    grad_attended = dot("ird,ed->ire", grad_branch, output_weight).astype(HALF)
    grad_attended = grad_attended.reshape(images, latent_rows, heads_here, HEAD)
    grad_probs = dot("irhc,ikhc->ihrk", grad_attended, value_heads)
    grad_scores = (probs * (grad_probs - jnp.sum(probs * grad_probs, -1, keepdims=True))).astype(
        HALF
    )
    grad_queries = (dot("ihrk,ikhc->irhc", grad_scores, key_heads) * factor).astype(HALF)
    grad_queries = grad_queries.reshape(images, latent_rows, inner_here)
    grad_keys = (dot("ihrk,irhc->ikhc", grad_scores, query_heads) * factor).astype(HALF)
    grad_keys = grad_keys.reshape(images, keys_all, inner_here)
    grad_values = dot("ihrk,irhc->ikhc", probs_low, grad_attended).astype(HALF)
    grad_values = grad_values.reshape(images, keys_all, inner_here)
    small = jnp.concatenate(
        [
            dot("ikd,ike->de", kv_input, grad_keys),
            dot("ikd,ike->de", kv_input, grad_values),
            dot("ird,ire->de", query_input, grad_queries),
            dot("ird,ire->de", grad_branch, attended),
        ],
        1,
    )
    small = links.halve(small.reshape(devices, -1, 4 * inner_here), 0, links.bits)
    grad_key, grad_value, grad_query, grad_output = jnp.split(small, 4, axis=1)

    heads_out = jnp.concatenate([grad_keys, grad_values], 2)
    heads_in = links.swap(heads_out.astype(SINGLE))
    heads_in = narrow(heads_in.reshape(-1, 2 * inner_here)).reshape(heads_out.shape)
    query_in = links.swap(grad_queries.astype(SINGLE))
    query_in = narrow(query_in.reshape(-1, inner_here)).reshape(grad_queries.shape)
    all_heads = jnp.concatenate([heads_out, heads_in], 2)
    weights_kv = jnp.concatenate([key_weight, value_weight, weights_other[:, inner_here:]], 1)
    weights_q = jnp.concatenate([query_weight, weights_other[:, :inner_here]], 1)
    grad_media_norm = dot("ike,de->ikd", all_heads[:, :patches], weights_kv)
    grad_latent_norm = dot("ike,de->ikd", all_heads[:, patches:], weights_kv) + dot(
        "ire,de->ird", jnp.concatenate([grad_queries, query_in], 2), weights_q
    )
    grad_media, grad_media_gain, grad_media_bias = norm_back(
        grad_media_norm, media_hat, media_inv, media_gain
    )
    grad_latent_in, grad_latent_gain, grad_latent_bias = norm_back(
        grad_latent_norm, latent_hat, latent_inv, latent_gain
    )
    grad_latents = grad_middle + grad_latent_in
    vectors = jnp.stack(
        [
            grad_media_gain,
            grad_media_bias,
            grad_latent_gain,
            grad_latent_bias,
            grad_feed_gain,
            grad_feed_bias,
        ]
    )
    vectors = vectors.reshape(6, devices, -1).transpose(1, 0, 2)
    vectors = links.halve(vectors, 0, links.bits)
    return (
        result,
        grad_media.astype(HALF),
        grad_latents.astype(HALF),
        grad_query,
        grad_key,
        grad_value,
        grad_output.T,
        grad_up,
        grad_down,
    ) + tuple(vectors[at] for at in range(6))


def solution(mesh):
    devices = mesh.shape["dp"]
    images = P("dp", None, None)
    columns = P(None, "tensor")
    lines = P("tensor", None)

    def body(*args):
        return local(*args, devices=devices)

    return jax.shard_map(
        body,
        mesh=mesh,
        in_specs=(images, P("dp"), images, images)
        + (columns, columns, columns, lines, columns, lines)
        + (P(),) * 6,
        out_specs=(images,) * 3
        + (P("dp", "tensor"),) * 3
        + (P("tensor", "dp"), P("dp", "tensor"), P("tensor", "dp"))
        + (P("dp"),) * 6,
        check_vma=False,
    )
```

```python
import functools

import jax
import jax.numpy as jnp
from jax import lax
from jax.experimental import pallas as pl
from jax.experimental.pallas import tpu as pltpu
from jax.sharding import PartitionSpec as P

HEAD = 64
PATCH = 576
SHORT = 256
GROUP = 4
LANES = 128
EPSILON = 1e-05
SINGLE = jnp.float32
HALF = jnp.bfloat16


def dot(left, right, left_axis=1, right_axis=0):
    return lax.dot_general(
        left, right, (((left_axis,), (right_axis,)), ((), ())), preferred_element_type=SINGLE
    )


def moments(values):
    mean = jnp.mean(values, -1, keepdims=True)
    center = values - mean
    inverse = lax.rsqrt(jnp.mean(center * center, -1, keepdims=True) + EPSILON)
    return mean, center, inverse


def norm_back(upstream, normed, inverse, gain):
    product = upstream * normed
    scaled = upstream * gain
    shift = jnp.mean(scaled, -1, keepdims=True)
    slope = jnp.mean(product * gain, -1, keepdims=True)
    return inverse * (scaled - shift - normed * slope), product


def row_sums(values):
    count, width = values.shape
    return jnp.sum(values.reshape(count // 8, 8, width), axis=0)


def head_rows(array, heads):
    column = lax.broadcasted_iota(jnp.int32, array.shape, 1) // HEAD
    return jnp.concatenate([jnp.where(column == h, array, 0) for h in range(heads)], 0)


def head_merge(blocks, heads):
    rows = blocks.shape[0] // heads
    total = None
    for h in range(heads):
        part = blocks[h * rows : (h + 1) * rows]
        column = lax.broadcasted_iota(jnp.int32, part.shape, 1) // HEAD
        part = jnp.where(column == h, part, 0)
        total = part if total is None else total + part
    return total


def exact_gelu(values):
    below = 0.5 * (1.0 + lax.erf(values * (0.5**0.5)))
    density = jnp.exp(values * values * -0.5) * 0.3989422804014327
    return values * below, below + values * density


def call(body, name, grid, ins, outs, scratch=(), prefetch=(), flops=0, cost=None):
    moved = sum(a.size * a.dtype.itemsize for a, _ in ins)
    shapes = [jax.ShapeDtypeStruct(s, d) for s, d, _ in outs]
    moved += sum(s.size * s.dtype.itemsize for s in shapes)
    return pl.pallas_call(
        body,
        out_shape=shapes,
        grid_spec=pltpu.PrefetchScalarGridSpec(
            num_scalar_prefetch=len(prefetch),
            grid=grid,
            in_specs=[s for _, s in ins],
            out_specs=[s for _, _, s in outs],
            scratch_shapes=list(scratch),
        ),
        cost_estimate=pl.CostEstimate(flops=flops, bytes_accessed=moved, transcendentals=0),
        name=name,
    )(*prefetch, *[a for a, _ in ins])


def whole(array):
    zeros = (0,) * array.ndim
    return array, pl.BlockSpec(array.shape, lambda *at: zeros)


def by_image(shape):
    rest = (0,) * (len(shape) - 1)
    return pl.BlockSpec((1,) + tuple(shape[1:]), lambda at, *_: (at,) + rest)


def by_rows(rows, width):
    return pl.BlockSpec((rows, width), lambda at, *_: (at, 0))


def attend_body(
    buckets_ref, media_ref, latent_ref, wq_ref, wk_ref, wv_ref, wo_ref,
    mg_ref, mb_ref, lg_ref, lb_ref,
    kv_ref, q_ref, k_ref, v_ref, p_ref, att_ref, branch_ref, mean_ref, inv_ref,
):
    patches = media_ref.shape[1]
    latent_rows = latent_ref.shape[1]
    inner = wq_ref.shape[1]
    heads = inner // HEAD
    chunk = patches // 3
    for at in range(3):
        rows = slice(at * chunk, (at + 1) * chunk)
        mean, center, inverse = moments(media_ref[0, rows].astype(SINGLE))
        mean_ref[0, rows] = mean
        inv_ref[0, rows] = inverse
        low = (center * inverse * mg_ref[...] + mb_ref[...]).astype(HALF)
        kv_ref[0, rows] = low
        k_ref[0, rows] = dot(low, wk_ref[...]).astype(HALF)
        v_ref[0, rows] = dot(low, wv_ref[...]).astype(HALF)
    rows = slice(patches, patches + latent_rows)
    _, center, inverse = moments(latent_ref[0].astype(SINGLE))
    low = (center * inverse * lg_ref[...] + lb_ref[...]).astype(HALF)
    kv_ref[0, rows] = low
    k_ref[0, rows] = dot(low, wk_ref[...]).astype(HALF)
    v_ref[0, rows] = dot(low, wv_ref[...]).astype(HALF)
    query = dot(low, wq_ref[...]).astype(HALF)
    q_ref[0] = query
    spread = head_rows(query * HALF(HEAD**-0.5), heads)
    scores = dot(spread, k_ref[0], 1, 1)
    count = SHORT + (PATCH - SHORT) * buckets_ref[pl.program_id(0)]
    column = lax.broadcasted_iota(jnp.int32, scores.shape, 1)
    scores = jnp.where((column < count) | (column >= patches), scores, -1e30)
    shifted = jnp.exp(scores - jnp.max(scores, -1, keepdims=True))
    probs = shifted / jnp.sum(shifted, -1, keepdims=True)
    p_ref[0] = probs
    attended = head_merge(dot(probs.astype(HALF), v_ref[0]), heads).astype(HALF)
    att_ref[0] = attended
    branch_ref[0] = dot(attended, wo_ref[...])


def attend(buckets, media, latents, wq, wk, wv, wo, vectors):
    images, patches, width = media.shape
    latent_rows = latents.shape[1]
    inner = wq.shape[1]
    keys_all = patches + latent_rows
    heads = inner // HEAD
    outs = [
        ((images, keys_all, width), HALF),
        ((images, latent_rows, inner), HALF),
        ((images, keys_all, inner), HALF),
        ((images, keys_all, inner), HALF),
        ((images, heads * latent_rows, keys_all), SINGLE),
        ((images, latent_rows, inner), HALF),
        ((images, latent_rows, width), SINGLE),
        ((images, patches, 1), SINGLE),
        ((images, patches, 1), SINGLE),
    ]
    return call(
        attend_body,
        "attend",
        (images,),
        [(media, by_image(media.shape)), (latents, by_image(latents.shape))]
        + [whole(a) for a in (wq, wk, wv, wo) + tuple(vectors)],
        [(s, d, by_image(s)) for s, d in outs],
        prefetch=(buckets,),
        flops=images * keys_all * width * inner * 5,
    )


def middle_body(core_ref, latent_ref, own_ref, far_ref, gain_ref, bias_ref, mid_ref, low_ref, send_ref):
    middle = latent_ref[...].astype(SINGLE) + (own_ref[...] + far_ref[...])
    mid_ref[...] = middle
    _, center, inverse = moments(middle)
    low = (center * inverse * gain_ref[...] + bias_ref[...]).astype(HALF)
    low_ref[...] = low
    half = low.shape[0] // 2

    @pl.when(core_ref[0] == 0)
    def _():
        send_ref[...] = low[:half].astype(SINGLE)

    @pl.when(core_ref[0] == 1)
    def _():
        send_ref[...] = low[half:].astype(SINGLE)


def feed_body(low_ref, cot_ref, up_ref, down_ref, hidden_ref, part_ref):
    half = up_ref.shape[1] // 2
    total = None
    for at in range(2):
        cols = slice(at * half, (at + 1) * half)
        value, slope = exact_gelu(dot(low_ref[...], up_ref[:, cols]))
        hidden_ref[:, cols] = value.astype(HALF)
        grad = (slope * dot(cot_ref[...], down_ref[cols], 1, 1)).astype(HALF)
        piece = dot(grad, up_ref[:, cols], 1, 1)
        total = piece if total is None else total + piece

    @pl.when(pl.program_id(0) == 0)
    def _():
        part_ref[...] = total

    @pl.when(pl.program_id(0) > 0)
    def _():
        part_ref[...] += total


def feed(low, cot, up, down):
    rows, width = low.shape
    hidden = up.shape[1]
    block = 512
    return call(
        feed_body,
        "feed",
        (hidden // block,),
        [
            whole(low),
            whole(cot),
            (up, pl.BlockSpec((width, block), lambda at: (0, at))),
            (down, pl.BlockSpec((block, width), lambda at: (at, 0))),
        ],
        [
            ((rows, hidden), HALF, pl.BlockSpec((rows, block), lambda at: (0, at))),
            ((rows, width), SINGLE, pl.BlockSpec((rows, width), lambda at: (0, 0))),
        ],
        flops=6 * rows * width * hidden,
    )


def wide_body(member_ref, *refs):
    feeds, cots = refs[0:4], refs[4:8]
    up_ref, down_ref = refs[8:10]
    fl_ref, cl_ref, hid_ref, gp_ref = refs[10:14]
    fbuf, cbuf, sems = refs[14:]
    rows = fbuf.shape[1]
    copies = []
    for at in range(4):
        first = pltpu.make_async_copy(feeds[at], fbuf.at[at], sems.at[0, at])
        second = pltpu.make_async_copy(cots[at], cbuf.at[at], sems.at[1, at])
        first.start()
        second.start()
        copies.append((first, second))
    for at in range(4):
        here = slice(at * rows, (at + 1) * rows)
        copies[at][0].wait()
        low = fbuf[at].astype(HALF)
        fl_ref[here] = low
        value, slope = exact_gelu(dot(low, up_ref[...]))
        hid_ref[here] = value.astype(HALF)
        copies[at][1].wait()
        low = cbuf[at].astype(HALF)
        cl_ref[here] = low
        gp_ref[here] = (slope * dot(low, down_ref[...], 1, 1)).astype(HALF)


def wide(member, feeds, cots, up, down):
    rows, width = feeds[0].shape
    piece = up.shape[1] // GROUP
    every = pl.BlockSpec(memory_space=pl.ANY)
    outs = [((4 * rows, width), HALF)] * 2 + [((4 * rows, piece), HALF)] * 2
    return call(
        wide_body,
        "wide",
        (1,),
        [(a, every) for a in feeds + cots]
        + [
            (up, pl.BlockSpec((width, piece), lambda at, m: (0, m[0]))),
            (down, pl.BlockSpec((piece, width), lambda at, m: (m[0], 0))),
        ],
        [(s, d, pl.BlockSpec(s, lambda at, m: (0, 0))) for s, d in outs],
        scratch=[
            pltpu.VMEM((4, rows, width), SINGLE),
            pltpu.VMEM((4, rows, width), SINGLE),
            pltpu.SemaphoreType.DMA((2, 4)),
        ],
        prefetch=(member,),
        flops=4 * 4 * rows * width * piece,
    )


def wide_grad_body(order_ref, place_ref, fl_ref, cl_ref, hid_ref, gp_ref, out_ref):
    share = out_ref.shape[1]
    piece = gp_ref.shape[1]
    block = order_ref[pl.program_id(0)]
    up = dot(fl_ref[...], gp_ref[...], 0, 0)
    down = dot(cl_ref[...], hid_ref[...], 0, 0)
    per = LANES // share
    for at in range(per):
        rows = slice(at * share, (at + 1) * share)
        spot = place_ref[block * per + at]
        out_ref[spot, :, :piece] = up[rows]
        out_ref[spot, :, piece:] = down[rows]


def wide_grad(order, place, fl, cl, hid, gp, devices):
    rows, width = fl.shape
    piece = gp.shape[1]
    blocks = order.shape[0]
    share = width // devices
    count = blocks * LANES // share
    column = pl.BlockSpec((rows, LANES), lambda at, o, p: (0, o[at]))
    shape = (count, share, 2 * piece)
    return call(
        wide_grad_body,
        "wide_grad",
        (blocks,),
        [(fl, column), (cl, column), whole(hid), whole(gp)],
        [(shape, SINGLE, pl.BlockSpec(shape, lambda at, o, p: (0, 0, 0)))],
        prefetch=(order, place),
        flops=4 * rows * blocks * LANES * piece,
    )[0]


def back_body(
    mid_ref, own_ref, far_ref, cot_ref, gain_ref, wo_ref, q_ref, k_ref, v_ref, p_ref,
    gm_ref, gb_ref, gkv_ref, gkv_send_ref, gq_ref, gq_send_ref, vec_ref,
):
    inner = wo_ref.shape[0]
    heads = inner // HEAD
    upstream = own_ref[...] + far_ref[...]
    _, center, inverse = moments(mid_ref[...])
    moved, product = norm_back(upstream, center * inverse, inverse, gain_ref[...])
    grad_middle = cot_ref[...].astype(SINGLE) + moved
    gm_ref[...] = grad_middle
    branch = grad_middle.astype(HALF)
    gb_ref[...] = branch
    sums = (row_sums(product), row_sums(upstream))

    @pl.when(pl.program_id(0) == 0)
    def _():
        vec_ref[0], vec_ref[1] = sums

    @pl.when(pl.program_id(0) > 0)
    def _():
        vec_ref[0] += sums[0]
        vec_ref[1] += sums[1]

    attended = head_rows(dot(branch, wo_ref[...], 1, 1).astype(HALF), heads)
    query = head_rows(q_ref[0] * HALF(HEAD**-0.5), heads)
    probs = p_ref[0]
    grad_probs = dot(attended, v_ref[0], 1, 1)
    inside = jnp.sum(probs * grad_probs, -1, keepdims=True)
    scores = (probs * (grad_probs - inside)).astype(HALF)
    grad_query = (head_merge(dot(scores, k_ref[0]), heads) * HEAD**-0.5).astype(HALF)
    gq_ref[0] = grad_query
    gq_send_ref[0] = grad_query.astype(SINGLE)
    grad_key = dot(scores, query, 0, 0).astype(HALF)
    gkv_ref[0, :, :inner] = grad_key
    gkv_send_ref[0, :, :inner] = grad_key.astype(SINGLE)
    grad_value = dot(probs.astype(HALF), attended, 0, 0).astype(HALF)
    gkv_ref[0, :, inner:] = grad_value
    gkv_send_ref[0, :, inner:] = grad_value.astype(SINGLE)


def back(middle, own, far, cot, gain, wo, q, k, v, p):
    images, latent_rows, inner = q.shape
    keys_all = k.shape[1]
    rows, width = middle.shape
    line = by_rows(latent_rows, width)
    outs = [
        ((rows, width), SINGLE, line),
        ((rows, width), HALF, line),
        ((images, keys_all, 2 * inner), HALF, by_image((images, keys_all, 2 * inner))),
        ((images, keys_all, 2 * inner), SINGLE, by_image((images, keys_all, 2 * inner))),
        ((images, latent_rows, inner), HALF, by_image(q.shape)),
        ((images, latent_rows, inner), SINGLE, by_image(q.shape)),
        ((2, 8, width), SINGLE, pl.BlockSpec((2, 8, width), lambda at: (0, 0, 0))),
    ]
    return call(
        back_body,
        "back",
        (images,),
        [(a, line) for a in (middle, own, far, cot)]
        + [whole(gain), whole(wo)]
        + [(a, by_image(a.shape)) for a in (q, k, v, p)],
        outs,
        flops=images * 10 * q.shape[1] * 4 * keys_all * inner,
    )


def small_grad_body(place_ref, kv_ref, gb_ref, gkv_ref, gq_ref, att_ref, send_ref, keep_ref, *, images, patches):
    share = send_ref.shape[1]
    inner = att_ref.shape[1]
    held = send_ref.shape[0]
    per = LANES // share
    keys_all = kv_ref.shape[0] // images
    latent = jnp.concatenate(
        [kv_ref[i * keys_all + patches : (i + 1) * keys_all] for i in range(images)], 0
    )
    pair = dot(kv_ref[...], gkv_ref[...], 0, 0)
    query = dot(latent, gq_ref[...], 0, 0)
    output = dot(gb_ref[...], att_ref[...], 0, 0)
    for at in range(per):
        rows = slice(at * share, (at + 1) * share)
        spot = place_ref[pl.program_id(0) * per + at]

        @pl.when(spot < held)
        def _():
            send_ref[spot, :, : 2 * inner] = pair[rows]
            send_ref[spot, :, 2 * inner : 3 * inner] = query[rows]
            send_ref[spot, :, 3 * inner :] = output[rows]

        @pl.when(spot >= held)
        def _():
            keep_ref[spot - held, :, : 2 * inner] = pair[rows]
            keep_ref[spot - held, :, 2 * inner : 3 * inner] = query[rows]
            keep_ref[spot - held, :, 3 * inner :] = output[rows]


def small_grad(place, kv, gb, gkv, gq, att, devices, images, patches):
    rows, width = kv.shape
    inner = att.shape[1]
    shape = (devices // 2, width // devices, 4 * inner)
    spec = pl.BlockSpec(shape, lambda at, p: (0, 0, 0))
    return call(
        functools.partial(small_grad_body, images=images, patches=patches),
        "small_grad",
        (width // LANES,),
        [
            (kv, pl.BlockSpec((rows, LANES), lambda at, p: (0, at))),
            (gb, pl.BlockSpec((gb.shape[0], LANES), lambda at, p: (0, at))),
        ]
        + [whole(a) for a in (gkv, gq, att)],
        [(shape, SINGLE, spec), (shape, SINGLE, spec)],
        prefetch=(place,),
        flops=4 * rows * width * inner,
    )


def inputs_body(
    gkv_ref, gkv_far_ref, gq_ref, gq_far_ref, media_ref, mean_ref, inv_ref, latent_ref, gm_ref,
    wq_ref, wk_ref, wv_ref, far_ref, mg_ref, lg_ref,
    out_ref, late_ref, vec_ref, heads_ref, query_ref,
):
    inner = wq_ref.shape[1]
    patches = media_ref.shape[1]

    @pl.when(pl.program_id(0) == 0)
    def _():
        heads_ref[:, :inner] = wk_ref[...]
        heads_ref[:, inner : 2 * inner] = wv_ref[...]
        heads_ref[:, 2 * inner :] = far_ref[:, inner:].astype(HALF)
        query_ref[:, :inner] = wq_ref[...]
        query_ref[:, inner:] = far_ref[:, :inner].astype(HALF)
        vec_ref[...] = jnp.zeros_like(vec_ref)

    chunk = patches // 3
    for at in range(3):
        rows = slice(at * chunk, (at + 1) * chunk)
        left = jnp.concatenate([gkv_ref[0, rows], gkv_far_ref[0, rows].astype(HALF)], 1)
        upstream = dot(left, heads_ref[...], 1, 1)
        inverse = inv_ref[0, rows]
        normed = (media_ref[0, rows].astype(SINGLE) - mean_ref[0, rows]) * inverse
        moved, product = norm_back(upstream, normed, inverse, mg_ref[...])
        out_ref[0, rows] = moved.astype(HALF)
        vec_ref[0] += row_sums(product)
        vec_ref[1] += row_sums(upstream)
    left = jnp.concatenate([gkv_ref[0, patches:], gkv_far_ref[0, patches:].astype(HALF)], 1)
    upstream = dot(left, heads_ref[...], 1, 1)
    left = jnp.concatenate([gq_ref[0], gq_far_ref[0].astype(HALF)], 1)
    upstream += dot(left, query_ref[...], 1, 1)
    _, center, inverse = moments(latent_ref[0].astype(SINGLE))
    moved, product = norm_back(upstream, center * inverse, inverse, lg_ref[...])
    late_ref[0] = (gm_ref[0] + moved).astype(HALF)
    vec_ref[2] += row_sums(product)
    vec_ref[3] += row_sums(upstream)


def inputs_back(gkv, gkv_far, gq, gq_far, media, mean, inv, latents, gm, wq, wk, wv, far, mg, lg):
    images, patches, width = media.shape
    inner = wq.shape[1]
    vec = (4, 8, width)
    return call(
        inputs_body,
        "inputs_back",
        (images,),
        [(a, by_image(a.shape)) for a in (gkv, gkv_far, gq, gq_far, media, mean, inv, latents, gm)]
        + [whole(a) for a in (wq, wk, wv, far, mg, lg)],
        [
            (media.shape, HALF, by_image(media.shape)),
            (latents.shape, HALF, by_image(latents.shape)),
            (vec, SINGLE, pl.BlockSpec(vec, lambda at: (0, 0, 0))),
        ],
        scratch=[pltpu.VMEM((width, 4 * inner), HALF), pltpu.VMEM((width, 2 * inner), HALF)],
        flops=8 * images * patches * width * inner,
    )


def place_body(member_ref, *refs):
    blocks, (up_ref, down_ref) = refs[:GROUP], refs[GROUP:]
    piece = blocks[0].shape[1] // 2
    for step in range(GROUP):
        spot = member_ref[0] ^ step
        up_ref[:, pl.ds(pl.multiple_of(spot * piece, piece), piece)] = blocks[step][:, :piece]
        down_ref[pl.ds(pl.multiple_of(spot * piece, piece), piece), :] = blocks[step][:, piece:].T


def place_pieces(member, blocks):
    share, both = blocks[0].shape
    wide_ = both // 2 * GROUP
    return call(
        place_body,
        "place_pieces",
        (1,),
        [whole(b) for b in blocks],
        [
            ((share, wide_), SINGLE, pl.BlockSpec((share, wide_), lambda at, m: (0, 0))),
            ((wide_, share), SINGLE, pl.BlockSpec((wide_, share), lambda at, m: (0, 0))),
        ],
        prefetch=(member,),
    )


class Links:
    def __init__(self, devices):
        self.devices = devices
        self.bits = devices.bit_length() - 1
        self.row = lax.axis_index("dp")
        self.core = lax.axis_index("tensor")

    def swap(self, array):
        return lax.ppermute(array, "tensor", [(0, 1), (1, 0)])

    def send(self, array, step_zero, step_one):
        pairs = []
        for row in range(self.devices):
            pairs.append((2 * row, 2 * (row ^ step_zero)))
            pairs.append((2 * row + 1, 2 * (row ^ step_one) + 1))
        return lax.ppermute(array, ("dp", "tensor"), pairs)

    def places(self, orders, tail):
        apart = jnp.arange(self.devices, dtype=jnp.int32) ^ self.row
        found = []
        for order in orders:
            spot = jnp.zeros_like(apart)
            for which in order:
                spot = 2 * spot + 1 - ((apart >> which) & 1)
            found.append(spot * (1 << tail) + apart % (1 << tail))
        return jnp.where(self.core == 0, found[0], found[1])

    def reduce(self, leave, keep, orders):
        for step, (zero, one) in enumerate(zip(*orders)):
            come = self.send(leave, 1 << zero, 1 << one)
            if step == len(orders[0]) - 1:
                return keep + come
            half = keep.shape[0] // 2
            leave, keep = keep[:half] + come[:half], keep[half:] + come[half:]

    def gather(self, own):
        near = self.send(own, 1, 2)
        pair = jnp.concatenate([own, near], 0)
        far = self.send(pair, 2, 1)
        return [pair, far, self.swap(pair), self.swap(far)]

    def total(self, array):
        for at in range(self.bits):
            array = array + self.send(array, 1 << at, 1 << at)
        return array


def local(
    media, buckets, latents, cotangent, query_weight, key_weight, value_weight, output_weight,
    up_weight, down_weight, media_gain, media_bias, latent_gain, latent_bias, feed_gain, feed_bias,
    devices,
):
    links = Links(devices)
    images, patches, width = media.shape
    latent_rows = latents.shape[1]
    rows = images * latent_rows
    inner = query_weight.shape[1]
    keys_all = patches + latent_rows
    share = width // devices
    vectors = [v.reshape(1, width) for v in (media_gain, media_bias, latent_gain, latent_bias)]
    gain, bias = feed_gain.reshape(1, width), feed_bias.reshape(1, width)
    core = links.core.reshape(1)
    member = (links.row % GROUP).reshape(1)

    cot = cotangent.reshape(rows, width)
    half = rows // 2
    cots = links.gather(
        lax.dynamic_slice_in_dim(cot, links.core * half, half, 0).astype(SINGLE)
    )
    weights_far = links.swap(
        jnp.concatenate([query_weight, key_weight, value_weight], 1).astype(SINGLE)
    )
    kv, q, k, v, probs, attended, branch, mean, inv = attend(
        buckets, media, latents, query_weight, key_weight, value_weight, output_weight, vectors
    )
    branch = branch.reshape(rows, width)
    middle, low, low_send = call(
        middle_body,
        "middle",
        (1,),
        [whole(a) for a in (latents.reshape(rows, width), branch, links.swap(branch), gain, bias)],
        [
            ((rows, width), SINGLE, pl.BlockSpec((rows, width), lambda at, c: (0, 0))),
            ((rows, width), HALF, pl.BlockSpec((rows, width), lambda at, c: (0, 0))),
            ((half, width), SINGLE, pl.BlockSpec((half, width), lambda at, c: (0, 0))),
        ],
        prefetch=(core,),
    )
    feeds = links.gather(low_send)
    hidden, part = feed(low, cot, up_weight, down_weight)
    grad_middle, grad_branch, gkv, gkv_send, gq, gq_send, feed_vec = back(
        middle, part, links.swap(part), cot, gain, output_weight, q, k, v, probs
    )
    gkv_far, gq_far = links.swap(gkv_send), links.swap(gq_send)

    bits = links.bits
    orders = [list(range(bits)), [1, 0] + list(range(2, bits))]
    if bits >= 4:
        orders[1][2:4] = [3, 2]
    leave, keep = small_grad(
        links.places(orders, 0),
        kv.reshape(images * keys_all, width),
        grad_branch,
        gkv.reshape(images * keys_all, 2 * inner),
        gq.reshape(rows, inner),
        attended.reshape(rows, inner),
        devices,
        images,
        patches,
    )
    small = links.reduce(leave, keep, orders)[0]

    fl, cl, hid, gp = wide(member, feeds, cots, up_weight, down_weight)
    top = bits - 1
    rest = list(range(2, top - 1))
    orders = [[top, top - 1] + rest, [top - 1, top] + rest]
    place = links.places(orders, 2)
    which = jnp.where(links.core == 0, top, top - 1)
    mine = (links.row >> which) & 1
    held = width // LANES // 2
    at = which - (bits - held.bit_length())
    rank = jnp.arange(held, dtype=jnp.int32)
    order = ((rank >> at) << (at + 1)) + (rank & ((1 << at) - 1))
    count = devices // 2
    leave = wide_grad(order + ((1 - mine) << at), place % count, fl, cl, hid, gp, devices)
    keep = wide_grad(order + (mine << at), place % count, fl, cl, hid, gp, devices)
    mixed = links.reduce(leave, keep, orders)
    pieces = [mixed[0]] + [links.send(mixed[s], s, s) for s in range(1, GROUP)]
    grad_up, grad_down = place_pieces(member, pieces)

    grad_media, grad_latents, vec = inputs_back(
        gkv, gkv_far, gq, gq_far, media, mean, inv, latents,
        grad_middle.reshape(images, latent_rows, width),
        query_weight, key_weight, value_weight, weights_far, vectors[0], vectors[2],
    )
    vec = jnp.sum(jnp.concatenate([vec, feed_vec], 0), 1)
    vec = links.total(jnp.concatenate([vec, jnp.zeros((2, width), SINGLE)], 0))
    vec = lax.dynamic_slice_in_dim(vec, links.row * share, share, 1)

    feed_out = dot(hidden, down_weight)
    result = (middle + (feed_out + links.swap(feed_out))).astype(HALF)
    return (
        result.reshape(latents.shape),
        grad_media,
        grad_latents,
        small[:, 2 * inner : 3 * inner],
        small[:, :inner],
        small[:, inner : 2 * inner],
        small[:, 3 * inner :].T,
        grad_up,
        grad_down,
    ) + tuple(vec[at] for at in range(6))


def solution(mesh):
    devices = mesh.shape["dp"]
    images = P("dp", None, None)
    columns = P(None, "tensor")
    lines = P("tensor", None)

    def body(*args):
        return local(*args, devices=devices)

    return jax.shard_map(
        body,
        mesh=mesh,
        in_specs=(images, P("dp"), images, images)
        + (columns, columns, columns, lines, columns, lines)
        + (P(),) * 6,
        out_specs=(images,) * 3
        + (P("dp", "tensor"),) * 3
        + (P("tensor", "dp"), P("dp", "tensor"), P("tensor", "dp"))
        + (P("dp"),) * 6,
        check_vma=False,
    )
```

```python
import functools

import jax
import jax.numpy as jnp
from jax import lax
from jax.experimental import pallas as pl
from jax.experimental.pallas import tpu as pltpu
from jax.sharding import PartitionSpec as P

HEAD = 64
PATCH = 576
SHORT = 256
GROUP = 4
LANES = 128
WIDE = 256
EPSILON = 1e-05
SINGLE = jnp.float32
HALF = jnp.bfloat16


def dot(left, right, left_axis=1, right_axis=0):
    return lax.dot_general(
        left, right, (((left_axis,), (right_axis,)), ((), ())), preferred_element_type=SINGLE
    )


def moments(values):
    mean = jnp.mean(values, -1, keepdims=True)
    center = values - mean
    inverse = lax.rsqrt(jnp.mean(center * center, -1, keepdims=True) + EPSILON)
    return mean, center, inverse


def norm_back(upstream, normed, inverse, gain):
    product = upstream * normed
    scaled = upstream * gain
    shift = jnp.mean(scaled, -1, keepdims=True)
    slope = jnp.mean(product * gain, -1, keepdims=True)
    return inverse * (scaled - shift - normed * slope), product


def row_sums(values):
    count, width = values.shape
    return jnp.sum(values.reshape(count // 8, 8, width), axis=0)


def head_rows(array, heads):
    column = lax.broadcasted_iota(jnp.int32, array.shape, 1) // HEAD
    return jnp.concatenate([jnp.where(column == h, array, 0) for h in range(heads)], 0)


def head_merge(blocks, heads):
    rows = blocks.shape[0] // heads
    total = None
    for h in range(heads):
        part = blocks[h * rows : (h + 1) * rows]
        column = lax.broadcasted_iota(jnp.int32, part.shape, 1) // HEAD
        part = jnp.where(column == h, part, 0)
        total = part if total is None else total + part
    return total


def exact_gelu(values):
    below = 0.5 * (1.0 + lax.erf(values * (0.5**0.5)))
    density = jnp.exp(values * values * -0.5) * 0.3989422804014327
    return values * below, below + values * density


def call(body, name, grid, ins, outs, scratch=(), prefetch=(), flops=0, aliases=None):
    moved = sum(a.size * a.dtype.itemsize for a, _ in ins)
    shapes = [jax.ShapeDtypeStruct(s, d) for s, d, _ in outs]
    moved += sum(s.size * s.dtype.itemsize for s in shapes)
    return pl.pallas_call(
        body,
        out_shape=shapes,
        grid_spec=pltpu.PrefetchScalarGridSpec(
            num_scalar_prefetch=len(prefetch),
            grid=grid,
            in_specs=[s for _, s in ins],
            out_specs=[s for _, _, s in outs],
            scratch_shapes=list(scratch),
        ),
        cost_estimate=pl.CostEstimate(flops=flops, bytes_accessed=moved, transcendentals=0),
        input_output_aliases=aliases or {},
        name=name,
    )(*prefetch, *[a for a, _ in ins])


def whole(array):
    zeros = (0,) * array.ndim
    return array, pl.BlockSpec(array.shape, lambda *at: zeros)


def by_image(shape):
    rest = (0,) * (len(shape) - 1)
    return pl.BlockSpec((1,) + tuple(shape[1:]), lambda at, *_: (at,) + rest)


def by_rows(rows, width):
    return pl.BlockSpec((rows, width), lambda at, *_: (at, 0))


def attend_body(
    buckets_ref, media_ref, latent_ref, wq_ref, wk_ref, wv_ref, wo_ref,
    mg_ref, mb_ref, lg_ref, lb_ref,
    kv_ref, q_ref, k_ref, v_ref, p_ref, att_ref, branch_ref, mean_ref, inv_ref,
):
    patches = media_ref.shape[1]
    latent_rows = latent_ref.shape[1]
    inner = wq_ref.shape[1]
    heads = inner // HEAD
    chunk = patches // 3
    for at in range(3):
        rows = slice(at * chunk, (at + 1) * chunk)
        mean, center, inverse = moments(media_ref[0, rows].astype(SINGLE))
        mean_ref[0, rows] = mean
        inv_ref[0, rows] = inverse
        low = (center * inverse * mg_ref[...] + mb_ref[...]).astype(HALF)
        kv_ref[0, rows] = low
        k_ref[0, rows] = dot(low, wk_ref[...]).astype(HALF)
        v_ref[0, rows] = dot(low, wv_ref[...]).astype(HALF)
    rows = slice(patches, patches + latent_rows)
    _, center, inverse = moments(latent_ref[0].astype(SINGLE))
    low = (center * inverse * lg_ref[...] + lb_ref[...]).astype(HALF)
    kv_ref[0, rows] = low
    k_ref[0, rows] = dot(low, wk_ref[...]).astype(HALF)
    v_ref[0, rows] = dot(low, wv_ref[...]).astype(HALF)
    query = dot(low, wq_ref[...]).astype(HALF)
    q_ref[0] = query
    spread = head_rows(query * HALF(HEAD**-0.5), heads)
    scores = dot(spread, k_ref[0], 1, 1)
    count = SHORT + (PATCH - SHORT) * buckets_ref[pl.program_id(0)]
    column = lax.broadcasted_iota(jnp.int32, scores.shape, 1)
    scores = jnp.where((column < count) | (column >= patches), scores, -1e30)
    shifted = jnp.exp(scores - jnp.max(scores, -1, keepdims=True))
    probs = shifted / jnp.sum(shifted, -1, keepdims=True)
    p_ref[0] = probs
    attended = head_merge(dot(probs.astype(HALF), v_ref[0]), heads).astype(HALF)
    att_ref[0] = attended
    branch_ref[0] = dot(attended, wo_ref[...])


def attend(buckets, media, latents, wq, wk, wv, wo, vectors):
    images, patches, width = media.shape
    latent_rows = latents.shape[1]
    inner = wq.shape[1]
    keys_all = patches + latent_rows
    heads = inner // HEAD
    outs = [
        ((images, keys_all, width), HALF),
        ((images, latent_rows, inner), HALF),
        ((images, keys_all, inner), HALF),
        ((images, keys_all, inner), HALF),
        ((images, heads * latent_rows, keys_all), SINGLE),
        ((images, latent_rows, inner), HALF),
        ((images, latent_rows, width), SINGLE),
        ((images, patches, 1), SINGLE),
        ((images, patches, 1), SINGLE),
    ]
    return call(
        attend_body,
        "attend",
        (images,),
        [(media, by_image(media.shape)), (latents, by_image(latents.shape))]
        + [whole(a) for a in (wq, wk, wv, wo) + tuple(vectors)],
        [(s, d, by_image(s)) for s, d in outs],
        prefetch=(buckets,),
        flops=images * keys_all * width * inner * 5,
    )


def middle_body(
    core_ref, latent_ref, own_ref, far_ref, gain_ref, bias_ref,
    mid_ref, low_ref, send_ref, first_ref, second_ref,
):
    middle = latent_ref[...].astype(SINGLE) + (own_ref[...] + far_ref[...])
    mid_ref[...] = middle
    _, center, inverse = moments(middle)
    low = (center * inverse * gain_ref[...] + bias_ref[...]).astype(HALF)
    low_ref[...] = low
    half = low.shape[0] // 2
    for which in range(2):

        @pl.when(core_ref[0] == which)
        def _():
            send = low[which * half : (which + 1) * half].astype(SINGLE)
            send_ref[...] = send
            first_ref[...] = send[: half // 2]
            second_ref[...] = send[half // 2 :]


def feed_body(low_ref, cot_ref, up_ref, down_ref, hidden_ref, grad_ref, part_ref, out_ref):
    half = up_ref.shape[1] // 2
    total, result = None, None
    for at in range(2):
        cols = slice(at * half, (at + 1) * half)
        value, slope = exact_gelu(dot(low_ref[...], up_ref[:, cols]))
        value = value.astype(HALF)
        hidden_ref[:, cols] = value
        grad = (slope * dot(cot_ref[...], down_ref[cols], 1, 1)).astype(HALF)
        grad_ref[:, cols] = grad
        piece = dot(grad, up_ref[:, cols], 1, 1)
        total = piece if total is None else total + piece
        piece = dot(value, down_ref[cols])
        result = piece if result is None else result + piece

    @pl.when(pl.program_id(0) == 0)
    def _():
        part_ref[...] = total
        out_ref[...] = result

    @pl.when(pl.program_id(0) > 0)
    def _():
        part_ref[...] += total
        out_ref[...] += result


def feed(low, cot, up, down):
    rows, width = low.shape
    hidden = up.shape[1]
    block = 512
    return call(
        feed_body,
        "feed",
        (hidden // block,),
        [
            whole(low),
            whole(cot),
            (up, pl.BlockSpec((width, block), lambda at: (0, at))),
            (down, pl.BlockSpec((block, width), lambda at: (at, 0))),
        ],
        [
            ((rows, hidden), HALF, pl.BlockSpec((rows, block), lambda at: (0, at))),
            ((rows, hidden), HALF, pl.BlockSpec((rows, block), lambda at: (0, at))),
            ((rows, width), SINGLE, pl.BlockSpec((rows, width), lambda at: (0, 0))),
            ((rows, width), SINGLE, pl.BlockSpec((rows, width), lambda at: (0, 0))),
        ],
        flops=8 * rows * width * hidden,
    )


def put_shares(value, place_ref, leave_ref, keep_ref):
    held, share = leave_ref.shape[:2]
    per = value.shape[0] // share
    for at in range(per):
        rows = value[at * share : (at + 1) * share]
        spot = place_ref[pl.program_id(0) * per + at]

        @pl.when(spot < held)
        def _():
            leave_ref[spot] = rows

        @pl.when(spot >= held)
        def _():
            keep_ref[spot - held] = rows


def down_side_body(member_ref, place_ref, *refs, counts):
    feeds, cots = refs[: counts[0]], refs[counts[0] : sum(counts)]
    up_ref, low_ref, cot_ref, own_ref = refs[sum(counts) :][:4]
    leave_ref, keep_ref, fl_ref, cl_ref, slope_ref = refs[sum(counts) + 4 :][:5]
    hid_ref, fbuf, cbuf, sems = refs[sum(counts) + 9 :]
    far = fbuf.shape[0]
    third = far // 3

    @pl.when(pl.program_id(0) == 0)
    def _():
        started = []
        for side, (arrays, buffer) in enumerate(((feeds, fbuf), (cots, cbuf))):
            first = 0
            for at, array in enumerate(arrays):
                count = array.shape[0]
                rows = pl.ds(first, count)
                copy = pltpu.make_async_copy(array, buffer.at[rows], sems.at[side, at])
                copy.start()
                started.append((copy, side, first))
                first += count
        for at in range(3):
            here = slice(at * third, (at + 1) * third)
            for copy, side, first in started:
                if side == 0 and here.start <= first < here.stop:
                    copy.wait()
            low = fbuf[here].astype(HALF)
            fl_ref[here] = low
            value, slope = exact_gelu(dot(low, up_ref[...]))
            hid_ref[here] = value.astype(HALF)
            slope_ref[here] = slope
        fl_ref[far:] = low_ref[...]
        hid_ref[far:] = own_ref[...]
        for copy, side, first in started:
            if side == 1:
                copy.wait()
        cl_ref[:far] = cbuf[...].astype(HALF)
        cl_ref[far:] = cot_ref[...]

    cols = pl.ds(pl.multiple_of(pl.program_id(0) * WIDE, WIDE), WIDE)
    put_shares(dot(cl_ref[:, cols], hid_ref[...], 0, 0), place_ref, leave_ref, keep_ref)


def down_side(member, place, feeds, cots, up, low, cot, hidden, devices):
    rows, width = low.shape
    far = 3 * rows
    total = far + rows
    counts = (len(feeds), len(cots))
    piece = up.shape[1] // GROUP
    every = pl.BlockSpec(memory_space=pl.ANY)
    shape = (devices // 2, width // devices, piece)
    fixed = [
        (shape, SINGLE), (shape, SINGLE), ((total, width), HALF), ((total, width), HALF),
        ((far, piece), SINGLE),
    ]
    return call(
        functools.partial(down_side_body, counts=counts),
        "down_side",
        (width // WIDE,),
        [(a, every) for a in feeds + cots]
        + [
            (up, pl.BlockSpec((width, piece), lambda at, m, p: (0, m[0]))),
            whole(low),
            whole(cot),
            (hidden, pl.BlockSpec((rows, piece), lambda at, m, p: (0, m[0]))),
        ],
        [(s, d, whole(jax.ShapeDtypeStruct(s, d))[1]) for s, d in fixed],
        scratch=[
            pltpu.VMEM((total, piece), HALF),
            pltpu.VMEM((far, width), SINGLE),
            pltpu.VMEM((far, width), SINGLE),
            pltpu.SemaphoreType.DMA((2, max(counts))),
        ],
        prefetch=(member, place),
    )


def up_side_body(
    member_ref, place_ref, fl_ref, cl_ref, slope_ref, down_ref, own_ref, leave_ref, keep_ref, gp_ref
):
    far = slope_ref.shape[0]
    third = far // 3

    @pl.when(pl.program_id(0) == 0)
    def _():
        for at in range(3):
            here = slice(at * third, (at + 1) * third)
            grad = slope_ref[here] * dot(cl_ref[here], down_ref[...], 1, 1)
            gp_ref[here] = grad.astype(HALF)
        gp_ref[far:] = own_ref[...]

    put_shares(dot(fl_ref[...], gp_ref[...], 0, 0), place_ref, leave_ref, keep_ref)


def up_side(member, place, fl, cl, slope, down, grad, devices):
    total, width = fl.shape
    far, piece = slope.shape
    rows = total - far
    shape = (devices // 2, width // devices, piece)
    spec = pl.BlockSpec(shape, lambda at, m, p: (0, 0, 0))
    return call(
        up_side_body,
        "up_side",
        (width // WIDE,),
        [
            (fl, pl.BlockSpec((total, WIDE), lambda at, m, p: (0, at))),
            (cl, pl.BlockSpec((far, width), lambda at, m, p: (0, 0))),
            whole(slope),
            (down, pl.BlockSpec((piece, width), lambda at, m, p: (m[0], 0))),
            (grad, pl.BlockSpec((rows, piece), lambda at, m, p: (0, m[0]))),
        ],
        [(shape, SINGLE, spec), (shape, SINGLE, spec)],
        scratch=[pltpu.VMEM((total, piece), HALF)],
        prefetch=(member, place),
    )


def back_body(
    mid_ref, own_ref, far_ref, cot_ref, gain_ref, wo_ref, q_ref, k_ref, v_ref, p_ref,
    gm_ref, gb_ref, gkv_ref, gkv_send_ref, gq_ref, gq_send_ref, vec_ref,
):
    inner = wo_ref.shape[0]
    heads = inner // HEAD
    upstream = own_ref[...] + far_ref[...]
    _, center, inverse = moments(mid_ref[...])
    moved, product = norm_back(upstream, center * inverse, inverse, gain_ref[...])
    grad_middle = cot_ref[...].astype(SINGLE) + moved
    gm_ref[...] = grad_middle
    branch = grad_middle.astype(HALF)
    gb_ref[...] = branch
    sums = (row_sums(product), row_sums(upstream))

    @pl.when(pl.program_id(0) == 0)
    def _():
        vec_ref[0], vec_ref[1] = sums

    @pl.when(pl.program_id(0) > 0)
    def _():
        vec_ref[0] += sums[0]
        vec_ref[1] += sums[1]

    attended = head_rows(dot(branch, wo_ref[...], 1, 1).astype(HALF), heads)
    query = head_rows(q_ref[0] * HALF(HEAD**-0.5), heads)
    probs = p_ref[0]
    grad_probs = dot(attended, v_ref[0], 1, 1)
    inside = jnp.sum(probs * grad_probs, -1, keepdims=True)
    scores = (probs * (grad_probs - inside)).astype(HALF)
    grad_query = (head_merge(dot(scores, k_ref[0]), heads) * HEAD**-0.5).astype(HALF)
    gq_ref[0] = grad_query
    gq_send_ref[0] = grad_query.astype(SINGLE)
    grad_key = dot(scores, query, 0, 0).astype(HALF)
    gkv_ref[0, :, :inner] = grad_key
    gkv_send_ref[0, :, :inner] = grad_key.astype(SINGLE)
    grad_value = dot(probs.astype(HALF), attended, 0, 0).astype(HALF)
    gkv_ref[0, :, inner:] = grad_value
    gkv_send_ref[0, :, inner:] = grad_value.astype(SINGLE)


def back(middle, own, far, cot, gain, wo, q, k, v, p):
    images, latent_rows, inner = q.shape
    keys_all = k.shape[1]
    rows, width = middle.shape
    line = by_rows(latent_rows, width)
    outs = [
        ((rows, width), SINGLE, line),
        ((rows, width), HALF, line),
        ((images, keys_all, 2 * inner), HALF, by_image((images, keys_all, 2 * inner))),
        ((images, keys_all, 2 * inner), SINGLE, by_image((images, keys_all, 2 * inner))),
        ((images, latent_rows, inner), HALF, by_image(q.shape)),
        ((images, latent_rows, inner), SINGLE, by_image(q.shape)),
        ((2, 8, width), SINGLE, pl.BlockSpec((2, 8, width), lambda at: (0, 0, 0))),
    ]
    return call(
        back_body,
        "back",
        (images,),
        [(a, line) for a in (middle, own, far, cot)]
        + [whole(gain), whole(wo)]
        + [(a, by_image(a.shape)) for a in (q, k, v, p)],
        outs,
        flops=images * 10 * q.shape[1] * 4 * keys_all * inner,
    )


def small_grad_body(place_ref, kv_ref, gb_ref, gkv_ref, gq_ref, att_ref, send_ref, keep_ref, *, images, patches):
    share = send_ref.shape[1]
    inner = att_ref.shape[1]
    held = send_ref.shape[0]
    per = LANES // share
    keys_all = kv_ref.shape[0] // images
    latent = jnp.concatenate(
        [kv_ref[i * keys_all + patches : (i + 1) * keys_all] for i in range(images)], 0
    )
    pair = dot(kv_ref[...], gkv_ref[...], 0, 0)
    query = dot(latent, gq_ref[...], 0, 0)
    output = dot(gb_ref[...], att_ref[...], 0, 0)
    for at in range(per):
        rows = slice(at * share, (at + 1) * share)
        spot = place_ref[pl.program_id(0) * per + at]

        @pl.when(spot < held)
        def _():
            send_ref[spot, :, : 2 * inner] = pair[rows]
            send_ref[spot, :, 2 * inner : 3 * inner] = query[rows]
            send_ref[spot, :, 3 * inner :] = output[rows]

        @pl.when(spot >= held)
        def _():
            keep_ref[spot - held, :, : 2 * inner] = pair[rows]
            keep_ref[spot - held, :, 2 * inner : 3 * inner] = query[rows]
            keep_ref[spot - held, :, 3 * inner :] = output[rows]


def small_grad(place, kv, gb, gkv, gq, att, devices, images, patches):
    rows, width = kv.shape
    inner = att.shape[1]
    shape = (devices // 2, width // devices, 4 * inner)
    spec = pl.BlockSpec(shape, lambda at, p: (0, 0, 0))
    return call(
        functools.partial(small_grad_body, images=images, patches=patches),
        "small_grad",
        (width // LANES,),
        [
            (kv, pl.BlockSpec((rows, LANES), lambda at, p: (0, at))),
            (gb, pl.BlockSpec((gb.shape[0], LANES), lambda at, p: (0, at))),
        ]
        + [whole(a) for a in (gkv, gq, att)],
        [(shape, SINGLE, spec), (shape, SINGLE, spec)],
        prefetch=(place,),
        flops=4 * rows * width * inner,
    )


def inputs_body(
    gkv_ref, gkv_far_ref, gq_ref, gq_far_ref, media_ref, mean_ref, inv_ref, latent_ref, gm_ref,
    wq_ref, wk_ref, wv_ref, far_ref, mg_ref, lg_ref,
    out_ref, late_ref, vec_ref, heads_ref, query_ref,
):
    inner = wq_ref.shape[1]
    patches = media_ref.shape[1]

    @pl.when(pl.program_id(0) == 0)
    def _():
        heads_ref[:, :inner] = wk_ref[...]
        heads_ref[:, inner : 2 * inner] = wv_ref[...]
        heads_ref[:, 2 * inner :] = far_ref[:, inner:].astype(HALF)
        query_ref[:, :inner] = wq_ref[...]
        query_ref[:, inner:] = far_ref[:, :inner].astype(HALF)
        vec_ref[...] = jnp.zeros_like(vec_ref)

    chunk = patches // 3
    for at in range(3):
        rows = slice(at * chunk, (at + 1) * chunk)
        left = jnp.concatenate([gkv_ref[0, rows], gkv_far_ref[0, rows].astype(HALF)], 1)
        upstream = dot(left, heads_ref[...], 1, 1)
        inverse = inv_ref[0, rows]
        normed = (media_ref[0, rows].astype(SINGLE) - mean_ref[0, rows]) * inverse
        moved, product = norm_back(upstream, normed, inverse, mg_ref[...])
        out_ref[0, rows] = moved.astype(HALF)
        vec_ref[0] += row_sums(product)
        vec_ref[1] += row_sums(upstream)
    left = jnp.concatenate([gkv_ref[0, patches:], gkv_far_ref[0, patches:].astype(HALF)], 1)
    upstream = dot(left, heads_ref[...], 1, 1)
    left = jnp.concatenate([gq_ref[0], gq_far_ref[0].astype(HALF)], 1)
    upstream += dot(left, query_ref[...], 1, 1)
    _, center, inverse = moments(latent_ref[0].astype(SINGLE))
    moved, product = norm_back(upstream, center * inverse, inverse, lg_ref[...])
    late_ref[0] = (gm_ref[0] + moved).astype(HALF)
    vec_ref[2] += row_sums(product)
    vec_ref[3] += row_sums(upstream)


def inputs_back(first, count, held, gkv, gkv_far, gq, gq_far, media, mean, inv, latents, gm, weights):
    images, patches, width = media.shape
    inner = weights[0].shape[1]
    vec = (4, 8, width)

    def image(array):
        rest = (0,) * (array.ndim - 1)
        return pl.BlockSpec((1,) + array.shape[1:], lambda at: (at + first,) + rest)

    arrays = (gkv, gkv_far, gq, gq_far, media, mean, inv, latents, gm)
    ins = [(a, image(a)) for a in arrays] + [whole(a) for a in weights]
    ins += [(a, pl.BlockSpec(memory_space=pl.ANY)) for a in held]
    body = inputs_body
    if held:
        def body(*refs):
            inputs_body(*refs[: len(arrays) + len(weights)], *refs[len(ins) :])

    return call(
        body,
        "inputs_back",
        (count,),
        ins,
        [
            (media.shape, HALF, image(media)),
            (latents.shape, HALF, image(latents)),
            (vec, SINGLE, pl.BlockSpec(vec, lambda at: (0, 0, 0))),
        ],
        scratch=[pltpu.VMEM((width, 4 * inner), HALF), pltpu.VMEM((width, 2 * inner), HALF)],
        flops=8 * count * patches * width * inner,
        aliases={len(ins) - len(held) + i: i for i in range(len(held))},
    )


def place_body(member_ref, *refs):
    blocks, out_ref = refs[:GROUP], refs[GROUP]
    piece = blocks[0].shape[1]
    for step in range(GROUP):
        spot = member_ref[0] ^ step
        out_ref[:, pl.ds(pl.multiple_of(spot * piece, piece), piece)] = blocks[step][...]


def place_pieces(member, blocks):
    share, piece = blocks[0].shape
    shape = (share, piece * GROUP)
    return call(
        place_body,
        "place_pieces",
        (1,),
        [whole(b) for b in blocks],
        [(shape, SINGLE, pl.BlockSpec(shape, lambda at, m: (0, 0)))],
        prefetch=(member,),
    )[0]


def after(array, *others):
    return lax.optimization_barrier((array,) + others)[0]


def plan(bits):
    if bits == 4:
        return (0, 3), ([1, 2], [2, 1]), ([0, 3, 2, 1], [2, 0, 1, 3])
    top = bits - 1
    rest = list(range(2, top - 1))
    wide_ = ([top, top - 1] + rest, [top - 1, top] + rest)
    return (0, 1), wide_, (list(range(bits)), [1, 0] + list(range(2, bits)))


class Links:
    def __init__(self, devices):
        self.devices = devices
        self.bits = devices.bit_length() - 1
        self.row = lax.axis_index("dp")
        self.core = lax.axis_index("tensor")

    def swap(self, array):
        return lax.ppermute(array, "tensor", [(0, 1), (1, 0)])

    def send(self, array, step_zero, step_one):
        pairs = []
        for row in range(self.devices):
            pairs.append((2 * row, 2 * (row ^ step_zero)))
            pairs.append((2 * row + 1, 2 * (row ^ step_one) + 1))
        return lax.ppermute(array, ("dp", "tensor"), pairs)

    def bit(self, which):
        return (self.row >> which) & 1

    def places(self, orders, group):
        apart = jnp.arange(self.devices, dtype=jnp.int32) ^ self.row
        found = []
        for order in orders:
            spot = jnp.zeros_like(apart)
            for which in order:
                spot = 2 * spot + 1 - ((apart >> which) & 1)
            for which in reversed(group):
                spot = 2 * spot + ((apart >> which) & 1)
            found.append(spot)
        return jnp.where(self.core == 0, found[0], found[1])

    def stage(self, leave, orders, step):
        return self.send(leave, 1 << orders[0][step], 1 << orders[1][step])

    def halve(self, come, keep):
        half = keep.shape[0] // 2
        return keep[:half] + come[:half], keep[half:] + come[half:]


def local(
    media, buckets, latents, cotangent, query_weight, key_weight, value_weight, output_weight,
    up_weight, down_weight, media_gain, media_bias, latent_gain, latent_bias, feed_gain, feed_bias,
    devices,
):
    links = Links(devices)
    images, patches, width = media.shape
    latent_rows = latents.shape[1]
    rows = images * latent_rows
    inner = query_weight.shape[1]
    keys_all = patches + latent_rows
    share = width // devices
    vectors = [v.reshape(1, width) for v in (media_gain, media_bias, latent_gain, latent_bias)]
    gain, bias = feed_gain.reshape(1, width), feed_bias.reshape(1, width)
    core = links.core.reshape(1)
    bits = links.bits
    group, wide_orders, small_orders = plan(bits)
    near_bit, far_bit = 1 << group[0], 1 << group[1]
    member = (links.bit(group[0]) + 2 * links.bit(group[1])).reshape(1)

    cot = cotangent.reshape(rows, width)
    half = rows // 2
    cot_own = lax.dynamic_slice_in_dim(cot, links.core * half, half, 0).astype(SINGLE)
    cot_far = links.send(cot_own, far_bit, far_bit)
    kv, q, k, v, probs, attended, branch, mean, inv = attend(
        buckets, media, latents, query_weight, key_weight, value_weight, output_weight, vectors
    )
    branch, cot_own, cot_far = lax.optimization_barrier((branch, cot_own, cot_far))
    branch = branch.reshape(rows, width)
    cot_near = links.send(cot_own, near_bit, near_bit)
    cot_far_other = links.swap(cot_far)
    branch_far = links.swap(branch)
    weights_send = jnp.concatenate(
        [after(query_weight, branch), key_weight, value_weight], 1
    ).astype(SINGLE)
    middle, low, low_send, low_first, low_second = call(
        middle_body,
        "middle",
        (1,),
        [
            whole(a)
            for a in (
                latents.reshape(rows, width),
                after(branch, weights_send),
                branch_far,
                gain,
                bias,
            )
        ],
        [
            ((rows, width), SINGLE, pl.BlockSpec((rows, width), lambda at, c: (0, 0))),
            ((rows, width), HALF, pl.BlockSpec((rows, width), lambda at, c: (0, 0))),
            ((half, width), SINGLE, pl.BlockSpec((half, width), lambda at, c: (0, 0))),
        ]
        + [((half // 2, width), SINGLE, pl.BlockSpec((half // 2, width), lambda at, c: (0, 0)))] * 2,
        prefetch=(core,),
    )
    low, low_send, low_first, cot_near, weights_send = lax.optimization_barrier(
        (low, low_send, low_first, cot_near, weights_send, cot_far_other)
    )[:5]
    low_far_a = links.send(low_first, far_bit, far_bit)
    low_near = links.send(low_send, near_bit, near_bit)
    cot_near_other = links.swap(cot_near)
    weights_far = links.swap(weights_send)
    hidden, grad_pre, part, feed_out = feed(low, cot, up_weight, down_weight)
    part, low_far_a, low_near, cot_far, low_second = lax.optimization_barrier(
        (part, low_far_a, low_near, cot_far, low_second, weights_far, cot_near_other)
    )[:5]
    part_far = links.swap(part)
    low_far_b = links.send(low_second, far_bit, far_bit)
    low_both_a = links.send(low_far_a, near_bit, near_bit)
    low_far_a_other = links.swap(low_far_a)
    cot_both = links.send(cot_far, near_bit, near_bit)
    grad_middle, grad_branch, gkv, gkv_send, gq, gq_send, feed_vec = back(
        middle, part, part_far, cot, gain, output_weight, q, k, v, probs
    )
    grad_branch, gkv_send, low_far_b, low_both_a, low_near, cot_both = lax.optimization_barrier(
        (grad_branch, gkv_send, low_far_b, low_both_a, low_near, cot_both, low_far_a_other)
    )[:6]
    low_both_b = links.send(low_far_b, near_bit, near_bit)
    low_far_b_other, low_both_a_other = links.swap(low_far_b), links.swap(low_both_a)
    gkv_far, low_near_other = links.swap(gkv_send), links.swap(low_near)
    small_leave, small_keep = small_grad(
        links.places(small_orders, ()),
        kv.reshape(images * keys_all, width),
        grad_branch,
        gkv.reshape(images * keys_all, 2 * inner),
        gq.reshape(rows, inner),
        attended.reshape(rows, inner),
        devices,
        images,
        patches,
    )
    small_leave, feed_out, gq_send, low_both_b, cot_both = lax.optimization_barrier(
        (
            small_leave, feed_out, gq_send, low_both_b, cot_both,
            low_far_b_other, low_both_a_other, gkv_far, low_near_other,
        )
    )[:5]
    low_both_b_other, cot_both_other = links.swap(low_both_b), links.swap(cot_both)
    small_come = links.stage(small_leave, small_orders, 0)
    gq_far, feed_far = links.swap(gq_send), links.swap(feed_out)
    place = links.places(wide_orders, group)
    down_leave, down_keep, fl, cl, slope = down_side(
        member,
        place,
        [
            low_near, low_near_other, low_far_a, low_far_b, low_far_a_other, low_far_b_other,
            low_both_a, low_both_b, low_both_a_other, low_both_b_other,
        ],
        [cot_near, cot_near_other, cot_far, cot_far_other, cot_both, cot_both_other],
        up_weight,
        low,
        cot,
        hidden,
        devices,
    )
    down_come = links.stage(down_leave, wide_orders, 0)
    up_leave, up_keep = up_side(
        member, place, fl, cl, slope, down_weight, after(grad_pre, down_leave), devices
    )
    up_come = links.stage(up_leave, wide_orders, 0)
    small_leave, small_keep = links.halve(
        small_come, after(small_keep, up_leave, gq_far, feed_far)
    )
    small_come = links.stage(small_leave, small_orders, 1)
    grad_media, grad_latents, vec = inputs_back(
        0,
        images,
        (),
        after(gkv, small_leave),
        gkv_far,
        gq,
        gq_far,
        media,
        mean,
        inv,
        latents,
        grad_middle.reshape(images, latent_rows, width),
        (query_weight, key_weight, value_weight, weights_far, vectors[0], vectors[2]),
    )
    vec = jnp.sum(jnp.concatenate([vec, feed_vec], 0), 1)
    vec = jnp.concatenate([vec, jnp.zeros((2, width), SINGLE)], 0)
    vec_steps = [1 << at for at in reversed(range(bits))]

    steps = len(wide_orders[0])
    done = vec
    for step in range(steps - 1):
        down_leave, down_keep = links.halve(down_come, after(down_keep, done))
        down_come = links.stage(down_leave, wide_orders, step + 1)
        up_leave, up_keep = links.halve(up_come, after(up_keep, down_leave))
        up_come = links.stage(up_leave, wide_orders, step + 1)
        done = up_leave
    vec_come = links.send(after(vec, done), vec_steps[0], vec_steps[0])
    for step in range(2, bits):
        small_leave, small_keep = links.halve(small_come, after(small_keep, done))
        small_come = links.stage(small_leave, small_orders, step)
        done = small_leave
        vec = after(vec, done) + vec_come
        vec_come = links.send(vec, vec_steps[step - 1], vec_steps[step - 1])
        if step == 2:
            result = (after(middle, done) + (feed_out + feed_far)).astype(HALF)
            done = result
            hops = [near_bit * (at & 1) + far_bit * (at >> 1) for at in range(GROUP)]
            mixed = after(down_keep, result) + down_come
            down_pieces = [mixed[0]] + [links.send(mixed[at], hops[at], hops[at]) for at in range(1, GROUP)]
            done = mixed
    mixed = after(up_keep, done) + up_come
    up_pieces = [mixed[0]] + [links.send(mixed[at], hops[at], hops[at]) for at in range(1, GROUP)]
    vec = after(vec, mixed) + vec_come
    vec = vec + links.send(vec, vec_steps[-1], vec_steps[-1])
    vec = lax.dynamic_slice_in_dim(vec, links.row * share, share, 1)
    small = (after(small_keep, vec) + small_come)[0]
    down_pieces[0] = after(down_pieces[0], small)
    grad_down = place_pieces(member, down_pieces)
    up_pieces[0] = after(up_pieces[0], grad_down)
    grad_up = place_pieces(member, up_pieces)
    return (
        result.reshape(latents.shape),
        grad_media,
        grad_latents,
        small[:, 2 * inner : 3 * inner],
        small[:, :inner],
        small[:, inner : 2 * inner],
        small[:, 3 * inner :].T,
        grad_up,
        grad_down.T,
    ) + tuple(vec[at] for at in range(6))


def solution(mesh):
    devices = mesh.shape["dp"]
    images = P("dp", None, None)
    columns = P(None, "tensor")
    lines = P("tensor", None)

    def body(*args):
        return local(*args, devices=devices)

    return jax.shard_map(
        body,
        mesh=mesh,
        in_specs=(images, P("dp"), images, images)
        + (columns, columns, columns, lines, columns, lines)
        + (P(),) * 6,
        out_specs=(images,) * 3
        + (P("dp", "tensor"),) * 3
        + (P("tensor", "dp"), P("dp", "tensor"), P("tensor", "dp"))
        + (P("dp"),) * 6,
        check_vma=False,
    )
```

```python
import functools

import jax
import jax.numpy as jnp
from jax import lax
from jax.experimental import pallas as pl
from jax.experimental.pallas import tpu as pltpu
from jax.sharding import PartitionSpec as P

HEAD = 64
PATCH = 576
SHORT = 256
GROUP = 4
LANES = 128
WIDE = 256
EPSILON = 1e-05
SINGLE = jnp.float32
HALF = jnp.bfloat16


def dot(left, right, left_axis=1, right_axis=0):
    return lax.dot_general(
        left, right, (((left_axis,), (right_axis,)), ((), ())), preferred_element_type=SINGLE
    )


def moments(values):
    mean = jnp.mean(values, -1, keepdims=True)
    center = values - mean
    inverse = lax.rsqrt(jnp.mean(center * center, -1, keepdims=True) + EPSILON)
    return mean, center, inverse


def norm_back(upstream, normed, inverse, gain):
    product = upstream * normed
    scaled = upstream * gain
    shift = jnp.mean(scaled, -1, keepdims=True)
    slope = jnp.mean(product * gain, -1, keepdims=True)
    return inverse * (scaled - shift - normed * slope), product


def row_sums(values):
    count, width = values.shape
    return jnp.sum(values.reshape(count // 8, 8, width), axis=0)


def head_rows(array, heads):
    column = lax.broadcasted_iota(jnp.int32, array.shape, 1) // HEAD
    return jnp.concatenate([jnp.where(column == h, array, 0) for h in range(heads)], 0)


def head_merge(blocks, heads):
    rows = blocks.shape[0] // heads
    total = None
    for h in range(heads):
        part = blocks[h * rows : (h + 1) * rows]
        column = lax.broadcasted_iota(jnp.int32, part.shape, 1) // HEAD
        part = jnp.where(column == h, part, 0)
        total = part if total is None else total + part
    return total


def exact_gelu(values):
    below = 0.5 * (1.0 + lax.erf(values * (0.5**0.5)))
    density = jnp.exp(values * values * -0.5) * 0.3989422804014327
    return values * below, below + values * density


def call(body, name, grid, ins, outs, scratch=(), prefetch=(), flops=0, aliases=None):
    moved = sum(a.size * a.dtype.itemsize for a, _ in ins)
    shapes = [jax.ShapeDtypeStruct(s, d) for s, d, _ in outs]
    moved += sum(s.size * s.dtype.itemsize for s in shapes)
    return pl.pallas_call(
        body,
        out_shape=shapes,
        grid_spec=pltpu.PrefetchScalarGridSpec(
            num_scalar_prefetch=len(prefetch),
            grid=grid,
            in_specs=[s for _, s in ins],
            out_specs=[s for _, _, s in outs],
            scratch_shapes=list(scratch),
        ),
        cost_estimate=pl.CostEstimate(flops=flops, bytes_accessed=moved, transcendentals=0),
        input_output_aliases=aliases or {},
        name=name,
    )(*prefetch, *[a for a, _ in ins])


def whole(array):
    zeros = (0,) * array.ndim
    return array, pl.BlockSpec(array.shape, lambda *at: zeros)


def by_image(shape):
    rest = (0,) * (len(shape) - 1)
    return pl.BlockSpec((1,) + tuple(shape[1:]), lambda at, *_: (at,) + rest)


def by_rows(rows, width):
    return pl.BlockSpec((rows, width), lambda at, *_: (at, 0))


def attend_body(
    buckets_ref, media_ref, latent_ref, wq_ref, wk_ref, wv_ref, wo_ref,
    mg_ref, mb_ref, lg_ref, lb_ref,
    kv_ref, q_ref, k_ref, v_ref, p_ref, att_ref, branch_ref, mean_ref, inv_ref,
):
    patches = media_ref.shape[1]
    latent_rows = latent_ref.shape[1]
    inner = wq_ref.shape[1]
    heads = inner // HEAD
    chunk = patches // 3
    for at in range(3):
        rows = slice(at * chunk, (at + 1) * chunk)
        mean, center, inverse = moments(media_ref[0, rows].astype(SINGLE))
        mean_ref[0, rows] = mean
        inv_ref[0, rows] = inverse
        low = (center * inverse * mg_ref[...] + mb_ref[...]).astype(HALF)
        kv_ref[0, rows] = low
        k_ref[0, rows] = dot(low, wk_ref[...]).astype(HALF)
        v_ref[0, rows] = dot(low, wv_ref[...]).astype(HALF)
    rows = slice(patches, patches + latent_rows)
    _, center, inverse = moments(latent_ref[0].astype(SINGLE))
    low = (center * inverse * lg_ref[...] + lb_ref[...]).astype(HALF)
    kv_ref[0, rows] = low
    k_ref[0, rows] = dot(low, wk_ref[...]).astype(HALF)
    v_ref[0, rows] = dot(low, wv_ref[...]).astype(HALF)
    query = dot(low, wq_ref[...]).astype(HALF)
    q_ref[0] = query
    spread = head_rows(query * HALF(HEAD**-0.5), heads)
    scores = dot(spread, k_ref[0], 1, 1)
    count = SHORT + (PATCH - SHORT) * buckets_ref[pl.program_id(0)]
    column = lax.broadcasted_iota(jnp.int32, scores.shape, 1)
    scores = jnp.where((column < count) | (column >= patches), scores, -1e30)
    shifted = jnp.exp(scores - jnp.max(scores, -1, keepdims=True))
    probs = shifted / jnp.sum(shifted, -1, keepdims=True)
    p_ref[0] = probs
    attended = head_merge(dot(probs.astype(HALF), v_ref[0]), heads).astype(HALF)
    att_ref[0] = attended
    branch_ref[0] = dot(attended, wo_ref[...])


def attend(buckets, media, latents, wq, wk, wv, wo, vectors):
    images, patches, width = media.shape
    latent_rows = latents.shape[1]
    inner = wq.shape[1]
    keys_all = patches + latent_rows
    heads = inner // HEAD
    outs = [
        ((images, keys_all, width), HALF),
        ((images, latent_rows, inner), HALF),
        ((images, keys_all, inner), HALF),
        ((images, keys_all, inner), HALF),
        ((images, heads * latent_rows, keys_all), SINGLE),
        ((images, latent_rows, inner), HALF),
        ((images, latent_rows, width), SINGLE),
        ((images, patches, 1), SINGLE),
        ((images, patches, 1), SINGLE),
    ]
    return call(
        attend_body,
        "attend",
        (images,),
        [(media, by_image(media.shape)), (latents, by_image(latents.shape))]
        + [whole(a) for a in (wq, wk, wv, wo) + tuple(vectors)],
        [(s, d, by_image(s)) for s, d in outs],
        prefetch=(buckets,),
        flops=images * keys_all * width * inner * 5,
    )


def middle_body(
    core_ref, latent_ref, own_ref, far_ref, gain_ref, bias_ref,
    mid_ref, low_ref, send_ref, first_ref, second_ref,
):
    middle = latent_ref[...].astype(SINGLE) + (own_ref[...] + far_ref[...])
    mid_ref[...] = middle
    _, center, inverse = moments(middle)
    low = (center * inverse * gain_ref[...] + bias_ref[...]).astype(HALF)
    low_ref[...] = low
    half = low.shape[0] // 2
    for which in range(2):

        @pl.when(core_ref[0] == which)
        def _():
            send = low[which * half : (which + 1) * half].astype(SINGLE)
            send_ref[...] = send
            first_ref[...] = send[: first_ref.shape[0]]
            second_ref[...] = send[first_ref.shape[0] :]


def feed_body(low_ref, cot_ref, up_ref, down_ref, hidden_ref, grad_ref, part_ref, out_ref):
    half = up_ref.shape[1] // 2
    total, result = None, None
    for at in range(2):
        cols = slice(at * half, (at + 1) * half)
        value, slope = exact_gelu(dot(low_ref[...], up_ref[:, cols]))
        value = value.astype(HALF)
        hidden_ref[:, cols] = value
        grad = (slope * dot(cot_ref[...], down_ref[cols], 1, 1)).astype(HALF)
        grad_ref[:, cols] = grad
        piece = dot(grad, up_ref[:, cols], 1, 1)
        total = piece if total is None else total + piece
        piece = dot(value, down_ref[cols])
        result = piece if result is None else result + piece

    @pl.when(pl.program_id(0) == 0)
    def _():
        part_ref[...] = total
        out_ref[...] = result

    @pl.when(pl.program_id(0) > 0)
    def _():
        part_ref[...] += total
        out_ref[...] += result


def feed(low, cot, up, down):
    rows, width = low.shape
    hidden = up.shape[1]
    block = 512
    return call(
        feed_body,
        "feed",
        (hidden // block,),
        [
            whole(low),
            whole(cot),
            (up, pl.BlockSpec((width, block), lambda at: (0, at))),
            (down, pl.BlockSpec((block, width), lambda at: (at, 0))),
        ],
        [
            ((rows, hidden), HALF, pl.BlockSpec((rows, block), lambda at: (0, at))),
            ((rows, hidden), HALF, pl.BlockSpec((rows, block), lambda at: (0, at))),
            ((rows, width), SINGLE, pl.BlockSpec((rows, width), lambda at: (0, 0))),
            ((rows, width), SINGLE, pl.BlockSpec((rows, width), lambda at: (0, 0))),
        ],
        flops=8 * rows * width * hidden,
    )


def put_shares(value, place_ref, leave_ref, keep_ref):
    held, share = leave_ref.shape[:2]
    per = value.shape[0] // share
    for at in range(per):
        rows = value[at * share : (at + 1) * share]
        spot = place_ref[pl.program_id(0) * per + at]

        @pl.when(spot < held)
        def _():
            leave_ref[spot] = rows

        @pl.when(spot >= held)
        def _():
            keep_ref[spot - held] = rows


def down_side_body(member_ref, place_ref, *refs, counts):
    feeds, cots = refs[: counts[0]], refs[counts[0] : sum(counts)]
    up_ref, low_ref, cot_ref, own_ref = refs[sum(counts) :][:4]
    leave_ref, keep_ref, fl_ref, cl_ref, slope_ref = refs[sum(counts) + 4 :][:5]
    hid_ref, fbuf, cbuf, sems = refs[sum(counts) + 9 :]
    far = fbuf.shape[0]
    third = far // 3

    @pl.when(pl.program_id(0) == 0)
    def _():
        started = []
        for side, (arrays, buffer) in enumerate(((feeds, fbuf), (cots, cbuf))):
            first = 0
            for at, array in enumerate(arrays):
                count = array.shape[0]
                rows = pl.ds(first, count)
                copy = pltpu.make_async_copy(array, buffer.at[rows], sems.at[side, at])
                copy.start()
                started.append((copy, side, first))
                first += count
        for at in range(3):
            here = slice(at * third, (at + 1) * third)
            for copy, side, first in started:
                if side == 0 and here.start <= first < here.stop:
                    copy.wait()
            low = fbuf[here].astype(HALF)
            fl_ref[here] = low
            value, slope = exact_gelu(dot(low, up_ref[...]))
            hid_ref[here] = value.astype(HALF)
            slope_ref[here] = slope
        fl_ref[far:] = low_ref[...]
        hid_ref[far:] = own_ref[...]
        for copy, side, first in started:
            if side == 1:
                copy.wait()
        cl_ref[:far] = cbuf[...].astype(HALF)
        cl_ref[far:] = cot_ref[...]

    cols = pl.ds(pl.multiple_of(pl.program_id(0) * WIDE, WIDE), WIDE)
    put_shares(dot(cl_ref[:, cols], hid_ref[...], 0, 0), place_ref, leave_ref, keep_ref)


def down_side(member, place, feeds, cots, up, low, cot, hidden, devices):
    rows, width = low.shape
    far = 3 * rows
    total = far + rows
    counts = (len(feeds), len(cots))
    piece = up.shape[1] // GROUP
    every = pl.BlockSpec(memory_space=pl.ANY)
    shape = (devices // 2, width // devices, piece)
    fixed = [
        (shape, SINGLE), (shape, SINGLE), ((total, width), HALF), ((total, width), HALF),
        ((far, piece), SINGLE),
    ]
    return call(
        functools.partial(down_side_body, counts=counts),
        "down_side",
        (width // WIDE,),
        [(a, every) for a in feeds + cots]
        + [
            (up, pl.BlockSpec((width, piece), lambda at, m, p: (0, m[0]))),
            whole(low),
            whole(cot),
            (hidden, pl.BlockSpec((rows, piece), lambda at, m, p: (0, m[0]))),
        ],
        [(s, d, whole(jax.ShapeDtypeStruct(s, d))[1]) for s, d in fixed],
        scratch=[
            pltpu.VMEM((total, piece), HALF),
            pltpu.VMEM((far, width), SINGLE),
            pltpu.VMEM((far, width), SINGLE),
            pltpu.SemaphoreType.DMA((2, max(counts))),
        ],
        prefetch=(member, place),
    )


def up_side_body(
    member_ref, place_ref, fl_ref, cl_ref, slope_ref, down_ref, own_ref, leave_ref, keep_ref, gp_ref
):
    far = slope_ref.shape[0]
    third = far // 3

    @pl.when(pl.program_id(0) == 0)
    def _():
        for at in range(3):
            here = slice(at * third, (at + 1) * third)
            grad = slope_ref[here] * dot(cl_ref[here], down_ref[...], 1, 1)
            gp_ref[here] = grad.astype(HALF)
        gp_ref[far:] = own_ref[...]

    put_shares(dot(fl_ref[...], gp_ref[...], 0, 0), place_ref, leave_ref, keep_ref)


def up_side(member, place, fl, cl, slope, down, grad, devices):
    total, width = fl.shape
    far, piece = slope.shape
    rows = total - far
    shape = (devices // 2, width // devices, piece)
    spec = pl.BlockSpec(shape, lambda at, m, p: (0, 0, 0))
    return call(
        up_side_body,
        "up_side",
        (width // WIDE,),
        [
            (fl, pl.BlockSpec((total, WIDE), lambda at, m, p: (0, at))),
            (cl, pl.BlockSpec((far, width), lambda at, m, p: (0, 0))),
            whole(slope),
            (down, pl.BlockSpec((piece, width), lambda at, m, p: (m[0], 0))),
            (grad, pl.BlockSpec((rows, piece), lambda at, m, p: (0, m[0]))),
        ],
        [(shape, SINGLE, spec), (shape, SINGLE, spec)],
        scratch=[pltpu.VMEM((total, piece), HALF)],
        prefetch=(member, place),
    )


def back_body(
    mid_ref, own_ref, far_ref, cot_ref, gain_ref, wo_ref, q_ref, k_ref, v_ref, p_ref,
    gm_ref, gb_ref, gkv_ref, gkv_send_ref, gq_ref, gq_send_ref, vec_ref,
):
    inner = wo_ref.shape[0]
    heads = inner // HEAD
    upstream = own_ref[...] + far_ref[...]
    _, center, inverse = moments(mid_ref[...])
    moved, product = norm_back(upstream, center * inverse, inverse, gain_ref[...])
    grad_middle = cot_ref[...].astype(SINGLE) + moved
    gm_ref[...] = grad_middle
    branch = grad_middle.astype(HALF)
    gb_ref[...] = branch
    sums = (row_sums(product), row_sums(upstream))

    @pl.when(pl.program_id(0) == 0)
    def _():
        vec_ref[0], vec_ref[1] = sums

    @pl.when(pl.program_id(0) > 0)
    def _():
        vec_ref[0] += sums[0]
        vec_ref[1] += sums[1]

    attended = head_rows(dot(branch, wo_ref[...], 1, 1).astype(HALF), heads)
    query = head_rows(q_ref[0] * HALF(HEAD**-0.5), heads)
    probs = p_ref[0]
    grad_probs = dot(attended, v_ref[0], 1, 1)
    inside = jnp.sum(probs * grad_probs, -1, keepdims=True)
    scores = (probs * (grad_probs - inside)).astype(HALF)
    grad_query = (head_merge(dot(scores, k_ref[0]), heads) * HEAD**-0.5).astype(HALF)
    gq_ref[0] = grad_query
    gq_send_ref[0] = grad_query.astype(SINGLE)
    grad_key = dot(scores, query, 0, 0).astype(HALF)
    gkv_ref[0, :, :inner] = grad_key
    gkv_send_ref[0, :, :inner] = grad_key.astype(SINGLE)
    grad_value = dot(probs.astype(HALF), attended, 0, 0).astype(HALF)
    gkv_ref[0, :, inner:] = grad_value
    gkv_send_ref[0, :, inner:] = grad_value.astype(SINGLE)


def back(middle, own, far, cot, gain, wo, q, k, v, p):
    images, latent_rows, inner = q.shape
    keys_all = k.shape[1]
    rows, width = middle.shape
    line = by_rows(latent_rows, width)
    outs = [
        ((rows, width), SINGLE, line),
        ((rows, width), HALF, line),
        ((images, keys_all, 2 * inner), HALF, by_image((images, keys_all, 2 * inner))),
        ((images, keys_all, 2 * inner), SINGLE, by_image((images, keys_all, 2 * inner))),
        ((images, latent_rows, inner), HALF, by_image(q.shape)),
        ((images, latent_rows, inner), SINGLE, by_image(q.shape)),
        ((2, 8, width), SINGLE, pl.BlockSpec((2, 8, width), lambda at: (0, 0, 0))),
    ]
    return call(
        back_body,
        "back",
        (images,),
        [(a, line) for a in (middle, own, far, cot)]
        + [whole(gain), whole(wo)]
        + [(a, by_image(a.shape)) for a in (q, k, v, p)],
        outs,
        flops=images * 10 * q.shape[1] * 4 * keys_all * inner,
    )


def small_grad_body(place_ref, kv_ref, gb_ref, gkv_ref, gq_ref, att_ref, send_ref, keep_ref, *, images, patches):
    share = send_ref.shape[1]
    inner = att_ref.shape[1]
    held = send_ref.shape[0]
    per = WIDE // share
    keys_all = kv_ref.shape[0] // images
    latent = jnp.concatenate(
        [kv_ref[i * keys_all + patches : (i + 1) * keys_all] for i in range(images)], 0
    )
    pair = dot(kv_ref[...], gkv_ref[...], 0, 0)
    query = dot(latent, gq_ref[...], 0, 0)
    output = dot(gb_ref[...], att_ref[...], 0, 0)
    for at in range(per):
        rows = slice(at * share, (at + 1) * share)
        spot = place_ref[pl.program_id(0) * per + at]

        @pl.when(spot < held)
        def _():
            send_ref[spot, :, : 2 * inner] = pair[rows]
            send_ref[spot, :, 2 * inner : 3 * inner] = query[rows]
            send_ref[spot, :, 3 * inner :] = output[rows]

        @pl.when(spot >= held)
        def _():
            keep_ref[spot - held, :, : 2 * inner] = pair[rows]
            keep_ref[spot - held, :, 2 * inner : 3 * inner] = query[rows]
            keep_ref[spot - held, :, 3 * inner :] = output[rows]


def small_grad(place, kv, gb, gkv, gq, att, devices, images, patches):
    rows, width = kv.shape
    inner = att.shape[1]
    shape = (devices // 2, width // devices, 4 * inner)
    spec = pl.BlockSpec(shape, lambda at, p: (0, 0, 0))
    return call(
        functools.partial(small_grad_body, images=images, patches=patches),
        "small_grad",
        (width // WIDE,),
        [
            (kv, pl.BlockSpec((rows, WIDE), lambda at, p: (0, at))),
            (gb, pl.BlockSpec((gb.shape[0], WIDE), lambda at, p: (0, at))),
        ]
        + [whole(a) for a in (gkv, gq, att)],
        [(shape, SINGLE, spec), (shape, SINGLE, spec)],
        prefetch=(place,),
        flops=4 * rows * width * inner,
    )


def inputs_body(
    gkv_ref, gkv_far_ref, gq_ref, gq_far_ref, media_ref, mean_ref, inv_ref, latent_ref, gm_ref,
    wq_ref, wk_ref, wv_ref, far_ref, mg_ref, lg_ref, before_ref,
    out_ref, late_ref, sums_ref, heads_ref, query_ref, vec_ref,
):
    inner = wq_ref.shape[1]
    patches = media_ref.shape[1]

    @pl.when(pl.program_id(0) == 0)
    def _():
        heads_ref[:, :inner] = wk_ref[...]
        heads_ref[:, inner : 2 * inner] = wv_ref[...]
        heads_ref[:, 2 * inner :] = far_ref[:, inner:].astype(HALF)
        query_ref[:, :inner] = wq_ref[...]
        query_ref[:, inner:] = far_ref[:, :inner].astype(HALF)
        vec_ref[...] = jnp.zeros_like(vec_ref)

    chunk = patches // 3
    for at in range(3):
        rows = slice(at * chunk, (at + 1) * chunk)
        left = jnp.concatenate([gkv_ref[0, rows], gkv_far_ref[0, rows].astype(HALF)], 1)
        upstream = dot(left, heads_ref[...], 1, 1)
        inverse = inv_ref[0, rows]
        normed = (media_ref[0, rows].astype(SINGLE) - mean_ref[0, rows]) * inverse
        moved, product = norm_back(upstream, normed, inverse, mg_ref[...])
        out_ref[0, rows] = moved.astype(HALF)
        vec_ref[0] += row_sums(product)
        vec_ref[1] += row_sums(upstream)
    left = jnp.concatenate([gkv_ref[0, patches:], gkv_far_ref[0, patches:].astype(HALF)], 1)
    upstream = dot(left, heads_ref[...], 1, 1)
    left = jnp.concatenate([gq_ref[0], gq_far_ref[0].astype(HALF)], 1)
    upstream += dot(left, query_ref[...], 1, 1)
    _, center, inverse = moments(latent_ref[0].astype(SINGLE))
    moved, product = norm_back(upstream, center * inverse, inverse, lg_ref[...])
    late_ref[0] = (gm_ref[0] + moved).astype(HALF)
    vec_ref[2] += row_sums(product)
    vec_ref[3] += row_sums(upstream)

    @pl.when(pl.program_id(0) == pl.num_programs(0) - 1)
    def _():
        for at in range(4):
            sums_ref[at : at + 1] = jnp.sum(vec_ref[at], 0, keepdims=True)
        if len(before_ref.shape) == 2:
            sums_ref[:4] += before_ref[:4]
            sums_ref[4:] = before_ref[4:]
        else:
            for at in range(2):
                sums_ref[at + 4 : at + 5] = jnp.sum(before_ref[at], 0, keepdims=True)
            sums_ref[6:] = jnp.zeros_like(sums_ref[6:])


def inputs_back(first, count, held, gkv, gkv_far, gq, gq_far, media, mean, inv, latents, gm, weights):
    images, patches, width = media.shape
    inner = weights[0].shape[1]
    vec = (8, width)

    def image(array):
        rest = (0,) * (array.ndim - 1)
        return pl.BlockSpec((1,) + array.shape[1:], lambda at: (at + first,) + rest)

    arrays = (gkv, gkv_far, gq, gq_far, media, mean, inv, latents, gm)
    ins = [(a, image(a)) for a in arrays] + [whole(a) for a in weights]
    ins += [(a, pl.BlockSpec(memory_space=pl.ANY)) for a in held]
    body = inputs_body
    if held:
        def body(*refs):
            inputs_body(*refs[: len(arrays) + len(weights)], *refs[len(ins) :])

    return call(
        body,
        "inputs_back",
        (count,),
        ins,
        [
            (media.shape, HALF, image(media)),
            (latents.shape, HALF, image(latents)),
            (vec, SINGLE, pl.BlockSpec(vec, lambda at: (0, 0))),
        ],
        scratch=[
            pltpu.VMEM((width, 4 * inner), HALF),
            pltpu.VMEM((width, 2 * inner), HALF),
            pltpu.VMEM((4, 8, width), SINGLE),
        ],
        flops=8 * count * patches * width * inner,
        aliases={len(ins) - len(held) + i: i for i in range(len(held))},
    )


def place_body(member_ref, *refs):
    blocks, out_ref = refs[:GROUP], refs[GROUP]
    piece = blocks[0].shape[1]
    for step in range(GROUP):
        spot = member_ref[0] ^ step
        out_ref[:, pl.ds(pl.multiple_of(spot * piece, piece), piece)] = blocks[step][...]


def place_pieces(member, blocks):
    share, piece = blocks[0].shape
    shape = (share, piece * GROUP)
    return call(
        place_body,
        "place_pieces",
        (1,),
        [whole(b) for b in blocks],
        [(shape, SINGLE, pl.BlockSpec(shape, lambda at, m: (0, 0)))],
        prefetch=(member,),
    )[0]


def after(array, *others):
    return lax.optimization_barrier((array,) + others)[0]


def plan(bits):
    if bits == 4:
        return (0, 3), ([1, 2], [2, 1]), ([0, 3, 1, 2], [1, 0, 2, 3])
    top = bits - 1
    rest = list(range(2, top - 1))
    wide_ = ([top, top - 1] + rest, [top - 1, top] + rest)
    return (0, 1), wide_, (list(range(bits)), [1, 0] + list(range(2, bits)))


class Links:
    def __init__(self, devices):
        self.devices = devices
        self.bits = devices.bit_length() - 1
        self.row = lax.axis_index("dp")
        self.core = lax.axis_index("tensor")

    def swap(self, array):
        return lax.ppermute(array, "tensor", [(0, 1), (1, 0)])

    def send(self, array, step_zero, step_one):
        pairs = []
        for row in range(self.devices):
            pairs.append((2 * row, 2 * (row ^ step_zero)))
            pairs.append((2 * row + 1, 2 * (row ^ step_one) + 1))
        return lax.ppermute(array, ("dp", "tensor"), pairs)

    def bit(self, which):
        return (self.row >> which) & 1

    def places(self, orders, group):
        apart = jnp.arange(self.devices, dtype=jnp.int32) ^ self.row
        found = []
        for order in orders:
            spot = jnp.zeros_like(apart)
            for which in order:
                spot = 2 * spot + 1 - ((apart >> which) & 1)
            for which in reversed(group):
                spot = 2 * spot + ((apart >> which) & 1)
            found.append(spot)
        return jnp.where(self.core == 0, found[0], found[1])

class Halving:
    def __init__(self, links, leave, keep, orders):
        self.links, self.keep, self.orders = links, keep, orders
        self.left = len(orders[0])
        self.send(leave)

    def send(self, leave):
        zero, one = self.orders
        self.come = self.links.send(leave, 1 << zero[-self.left], 1 << one[-self.left])

    def advance(self, *done):
        keep = after(self.keep, *done)
        self.left -= 1
        if not self.left:
            return keep + self.come
        half = keep.shape[0] // 2
        leave, self.keep = keep[:half] + self.come[:half], keep[half:] + self.come[half:]
        self.send(leave)
        return leave


class Total:
    def __init__(self, links, array, order):
        self.links, self.array, self.order = links, array, list(order)
        self.send()

    def send(self):
        hop = 1 << self.order.pop(0)
        self.come = self.links.send(self.array, hop, hop)

    def advance(self, *done):
        self.array = after(self.array, *done) + self.come
        if self.order:
            self.send()
        return self.array


def local(
    media, buckets, latents, cotangent, query_weight, key_weight, value_weight, output_weight,
    up_weight, down_weight, media_gain, media_bias, latent_gain, latent_bias, feed_gain, feed_bias,
    devices,
):
    links = Links(devices)
    images, patches, width = media.shape
    latent_rows = latents.shape[1]
    rows = images * latent_rows
    inner = query_weight.shape[1]
    keys_all = patches + latent_rows
    share = width // devices
    vectors = [v.reshape(1, width) for v in (media_gain, media_bias, latent_gain, latent_bias)]
    gain, bias = feed_gain.reshape(1, width), feed_bias.reshape(1, width)
    core = links.core.reshape(1)
    bits = links.bits
    group, wide_orders, small_orders = plan(bits)
    near_bit, far_bit = 1 << group[0], 1 << group[1]
    member = (links.bit(group[0]) + 2 * links.bit(group[1])).reshape(1)

    cot = cotangent.reshape(rows, width)
    half = rows // 2
    cot_own = lax.dynamic_slice_in_dim(cot, links.core * half, half, 0).astype(SINGLE)
    cut = half // 8 * 5
    cot_far_a = links.send(cot_own[:cut], far_bit, far_bit)
    cot_near = links.send(cot_own, near_bit, near_bit)
    kv, q, k, v, probs, attended, branch, mean, inv = attend(
        buckets, media, latents, query_weight, key_weight, value_weight, output_weight, vectors
    )
    branch, cot_own, cot_near, cot_far_a = lax.optimization_barrier(
        (branch, cot_own, cot_near, cot_far_a)
    )
    branch = branch.reshape(rows, width)
    cot_far_b = links.send(cot_own[cut:], far_bit, far_bit)
    cot_both_a = links.send(cot_far_a, near_bit, near_bit)
    cot_near_other = links.swap(cot_near)
    branch_far = links.swap(branch)
    weights_send = jnp.concatenate(
        [after(query_weight, branch), key_weight, value_weight], 1
    ).astype(SINGLE)
    middle, low, low_send, low_first, low_second = call(
        middle_body,
        "middle",
        (1,),
        [
            whole(a)
            for a in (
                latents.reshape(rows, width),
                after(branch, weights_send),
                branch_far,
                gain,
                bias,
            )
        ],
        [
            ((rows, width), SINGLE, pl.BlockSpec((rows, width), lambda at, c: (0, 0))),
            ((rows, width), HALF, pl.BlockSpec((rows, width), lambda at, c: (0, 0))),
            ((half, width), SINGLE, pl.BlockSpec((half, width), lambda at, c: (0, 0))),
        ]
        + [((r, width), SINGLE, pl.BlockSpec((r, width), lambda at, c: (0, 0))) for r in (half - cut, cut)],
        prefetch=(core,),
    )
    low, low_send, low_first, weights_send, cot_far_a, cot_far_b, cot_both_a = lax.optimization_barrier(
        (low, low_send, low_first, weights_send, cot_far_a, cot_far_b, cot_both_a, cot_near_other)
    )[:7]
    low_far_a = links.send(low_first, far_bit, far_bit)
    cot_both_b = links.send(cot_far_b, near_bit, near_bit)
    cot_far_a_other, cot_both_a_other = links.swap(cot_far_a), links.swap(cot_both_a)
    cot_far_b_other = links.swap(cot_far_b)
    hidden, grad_pre, part, feed_out = feed(low, cot, up_weight, down_weight)
    part, low_far_a, low_send, low_second, weights_send, cot_both_b = lax.optimization_barrier(
        (
            part, low_far_a, low_send, low_second, weights_send, cot_both_b,
            cot_far_a_other, cot_both_a_other, cot_far_b_other,
        )
    )[:6]
    part_far = links.swap(part)
    low_far_b = links.send(low_second, far_bit, far_bit)
    low_near = links.send(low_send, near_bit, near_bit)
    low_both_a = links.send(low_far_a, near_bit, near_bit)
    low_far_a_other = links.swap(low_far_a)
    cot_both_b_other = links.swap(cot_both_b)
    grad_middle, grad_branch, gkv, gkv_send, gq, gq_send, feed_vec = back(
        middle, part, part_far, cot, gain, output_weight, q, k, v, probs
    )
    grad_branch, gkv_send, low_near, low_far_b, low_both_a = lax.optimization_barrier(
        (
            grad_branch, gkv_send, low_near, low_far_b, low_both_a,
            low_far_a_other, cot_both_b_other,
        )
    )[:5]
    low_both_b = links.send(low_far_b, near_bit, near_bit)
    gkv_far = links.swap(gkv_send)
    low_near_other, low_far_b_other = links.swap(low_near), links.swap(low_far_b)
    low_both_a_other = links.swap(low_both_a)
    small_leave, small_keep = small_grad(
        links.places(small_orders, ()),
        kv.reshape(images * keys_all, width),
        grad_branch,
        gkv.reshape(images * keys_all, 2 * inner),
        gq.reshape(rows, inner),
        attended.reshape(rows, inner),
        devices,
        images,
        patches,
    )
    small_leave, low_both_b, gq_send, feed_out, weights_send = lax.optimization_barrier(
        (
            small_leave, low_both_b, gq_send, feed_out, weights_send,
            gkv_far, low_near_other, low_far_b_other, low_both_a_other,
        )
    )[:5]
    low_both_b_other = links.swap(low_both_b)
    small = Halving(links, small_leave, small_keep, small_orders)
    weights_far, gq_far = links.swap(weights_send), links.swap(gq_send)
    feed_far = links.swap(feed_out)
    place = links.places(wide_orders, group)
    down_leave, down_keep, fl, cl, slope = down_side(
        member,
        place,
        [
            low_near, low_near_other, low_far_a, low_far_b, low_far_a_other, low_far_b_other,
            low_both_a, low_both_b, low_both_a_other, low_both_b_other,
        ],
        [
            cot_near, cot_near_other, cot_far_a, cot_far_b, cot_far_a_other, cot_far_b_other,
            cot_both_a, cot_both_b, cot_both_a_other, cot_both_b_other,
        ],
        up_weight,
        low,
        cot,
        hidden,
        devices,
    )
    down = Halving(links, down_leave, down_keep, wide_orders)
    up_leave, up_keep = up_side(
        member,
        place,
        fl,
        cl,
        slope,
        down_weight,
        after(grad_pre, down_leave, weights_far, gq_far, feed_far),
        devices,
    )
    up = Halving(links, up_leave, up_keep, wide_orders)
    done = down.advance(small.advance(up_leave))
    inputs = (gkv_far, gq, gq_far, media, mean, inv, latents)
    inputs += (grad_middle.reshape(images, latent_rows, width),)
    weights = (query_weight, key_weight, value_weight, weights_far, vectors[0], vectors[2])
    part = images // 2
    early = inputs_back(0, part, (), after(gkv, done), *inputs, weights + (feed_vec,))

    hops = [near_bit * (at & 1) + far_bit * (at >> 1) for at in range(GROUP)]

    def pieces(mixed):
        return [mixed[0]] + [links.send(mixed[at], hops[at], hops[at]) for at in range(1, GROUP)]

    done = early[2]
    while down.left > 1:
        done = down.advance(done)
    mixed = down.advance(done)
    down_pieces = pieces(mixed)
    done = mixed
    while up.left > 1:
        done = up.advance(done)
    grad_media, grad_latents, vec = inputs_back(
        part, images - part, early[:2], after(gkv, done), *inputs, weights + (early[2],)
    )
    down_pieces = list(lax.optimization_barrier(tuple(down_pieces) + (vec,)))
    vec = down_pieces.pop()
    mixed = up.advance(vec)
    up_pieces = pieces(mixed)
    vec = Total(links, after(vec, mixed), [group[1], group[0]] + wide_orders[0])
    done = small.advance(vec.array)
    done = vec.advance(done, up_pieces[1])
    done = result = (after(middle, done) + (feed_out + feed_far)).astype(HALF)
    down_pieces[0] = after(down_pieces[0], done)
    done = grad_down = place_pieces(member, down_pieces)
    while small.left > 1:
        done = small.advance(done)
    done = vec.advance(done, up_pieces[2])
    done = vec.advance(done, up_pieces[3])
    while vec.order:
        done = vec.advance(done)
    vec = vec.advance(done)
    vec = lax.dynamic_slice_in_dim(vec, links.row * share, share, 1)
    up_pieces[0] = after(up_pieces[0], vec)
    grad_up = place_pieces(member, up_pieces)
    small = small.advance(grad_up)[0]
    return (
        result.reshape(latents.shape),
        grad_media,
        grad_latents,
        small[:, 2 * inner : 3 * inner],
        small[:, :inner],
        small[:, inner : 2 * inner],
        small[:, 3 * inner :].T,
        grad_up,
        grad_down.T,
    ) + tuple(vec[at] for at in range(6))


def solution(mesh):
    devices = mesh.shape["dp"]
    images = P("dp", None, None)
    columns = P(None, "tensor")
    lines = P("tensor", None)

    def body(*args):
        return local(*args, devices=devices)

    return jax.shard_map(
        body,
        mesh=mesh,
        in_specs=(images, P("dp"), images, images)
        + (columns, columns, columns, lines, columns, lines)
        + (P(),) * 6,
        out_specs=(images,) * 3
        + (P("dp", "tensor"),) * 3
        + (P("tensor", "dp"), P("dp", "tensor"), P("tensor", "dp"))
        + (P("dp"),) * 6,
        check_vma=False,
    )
```

```python
import functools

import jax
import jax.numpy as jnp
from jax import lax
from jax.experimental import pallas as pl
from jax.experimental.pallas import tpu as pltpu
from jax.sharding import PartitionSpec as P

HEAD = 64
PATCH = 576
SHORT = 256
GROUP = 4
LANES = 128
WIDE = 256
EPSILON = 1e-05
SINGLE = jnp.float32
HALF = jnp.bfloat16


def dot(left, right, left_axis=1, right_axis=0):
    return lax.dot_general(
        left, right, (((left_axis,), (right_axis,)), ((), ())), preferred_element_type=SINGLE
    )


def moments(values):
    mean = jnp.mean(values, -1, keepdims=True)
    center = values - mean
    inverse = lax.rsqrt(jnp.mean(center * center, -1, keepdims=True) + EPSILON)
    return mean, center, inverse


def norm_back(upstream, normed, inverse, gain):
    product = upstream * normed
    scaled = upstream * gain
    shift = jnp.mean(scaled, -1, keepdims=True)
    slope = jnp.mean(product * gain, -1, keepdims=True)
    return inverse * (scaled - shift - normed * slope), product


def row_sums(values):
    count, width = values.shape
    return jnp.sum(values.reshape(count // 8, 8, width), axis=0)


def head_rows(array, heads):
    column = lax.broadcasted_iota(jnp.int32, array.shape, 1) // HEAD
    return jnp.concatenate([jnp.where(column == h, array, 0) for h in range(heads)], 0)


def head_merge(blocks, heads):
    rows = blocks.shape[0] // heads
    total = None
    for h in range(heads):
        part = blocks[h * rows : (h + 1) * rows]
        column = lax.broadcasted_iota(jnp.int32, part.shape, 1) // HEAD
        part = jnp.where(column == h, part, 0)
        total = part if total is None else total + part
    return total


def exact_gelu(values):
    below = 0.5 * (1.0 + lax.erf(values * (0.5**0.5)))
    density = jnp.exp(values * values * -0.5) * 0.3989422804014327
    return values * below, below + values * density


def call(body, name, grid, ins, outs, scratch=(), prefetch=(), flops=0, aliases=None):
    moved = sum(a.size * a.dtype.itemsize for a, _ in ins)
    shapes = [jax.ShapeDtypeStruct(s, d) for s, d, _ in outs]
    moved += sum(s.size * s.dtype.itemsize for s in shapes)
    return pl.pallas_call(
        body,
        out_shape=shapes,
        grid_spec=pltpu.PrefetchScalarGridSpec(
            num_scalar_prefetch=len(prefetch),
            grid=grid,
            in_specs=[s for _, s in ins],
            out_specs=[s for _, _, s in outs],
            scratch_shapes=list(scratch),
        ),
        cost_estimate=pl.CostEstimate(flops=flops, bytes_accessed=moved, transcendentals=0),
        input_output_aliases=aliases or {},
        name=name,
    )(*prefetch, *[a for a, _ in ins])


def whole(array):
    zeros = (0,) * array.ndim
    return array, pl.BlockSpec(array.shape, lambda *at: zeros)


def by_image(shape):
    rest = (0,) * (len(shape) - 1)
    return pl.BlockSpec((1,) + tuple(shape[1:]), lambda at, *_: (at,) + rest)


def by_rows(rows, width):
    return pl.BlockSpec((rows, width), lambda at, *_: (at, 0))


def attend_body(
    buckets_ref, media_ref, latent_ref, wq_ref, wk_ref, wv_ref, wo_ref,
    mg_ref, mb_ref, lg_ref, lb_ref,
    kv_ref, q_ref, k_ref, v_ref, p_ref, att_ref, branch_ref, mean_ref, inv_ref,
):
    patches = media_ref.shape[1]
    latent_rows = latent_ref.shape[1]
    inner = wq_ref.shape[1]
    heads = inner // HEAD
    chunk = patches // 3
    for at in range(3):
        rows = slice(at * chunk, (at + 1) * chunk)
        mean, center, inverse = moments(media_ref[0, rows].astype(SINGLE))
        mean_ref[0, rows] = mean
        inv_ref[0, rows] = inverse
        low = (center * inverse * mg_ref[...] + mb_ref[...]).astype(HALF)
        kv_ref[0, rows] = low
        k_ref[0, rows] = dot(low, wk_ref[...]).astype(HALF)
        v_ref[0, rows] = dot(low, wv_ref[...]).astype(HALF)
    rows = slice(patches, patches + latent_rows)
    _, center, inverse = moments(latent_ref[0].astype(SINGLE))
    low = (center * inverse * lg_ref[...] + lb_ref[...]).astype(HALF)
    kv_ref[0, rows] = low
    k_ref[0, rows] = dot(low, wk_ref[...]).astype(HALF)
    v_ref[0, rows] = dot(low, wv_ref[...]).astype(HALF)
    query = dot(low, wq_ref[...]).astype(HALF)
    q_ref[0] = query
    spread = head_rows(query * HALF(HEAD**-0.5), heads)
    scores = dot(spread, k_ref[0], 1, 1)
    count = SHORT + (PATCH - SHORT) * buckets_ref[pl.program_id(0)]
    column = lax.broadcasted_iota(jnp.int32, scores.shape, 1)
    scores = jnp.where((column < count) | (column >= patches), scores, -1e30)
    shifted = jnp.exp(scores - jnp.max(scores, -1, keepdims=True))
    probs = shifted / jnp.sum(shifted, -1, keepdims=True)
    p_ref[0] = probs
    attended = head_merge(dot(probs.astype(HALF), v_ref[0]), heads).astype(HALF)
    att_ref[0] = attended
    branch_ref[0] = dot(attended, wo_ref[...])


def attend(buckets, media, latents, wq, wk, wv, wo, vectors):
    images, patches, width = media.shape
    latent_rows = latents.shape[1]
    inner = wq.shape[1]
    keys_all = patches + latent_rows
    heads = inner // HEAD
    outs = [
        ((images, keys_all, width), HALF),
        ((images, latent_rows, inner), HALF),
        ((images, keys_all, inner), HALF),
        ((images, keys_all, inner), HALF),
        ((images, heads * latent_rows, keys_all), SINGLE),
        ((images, latent_rows, inner), HALF),
        ((images, latent_rows, width), SINGLE),
        ((images, patches, 1), SINGLE),
        ((images, patches, 1), SINGLE),
    ]
    return call(
        attend_body,
        "attend",
        (images,),
        [(media, by_image(media.shape)), (latents, by_image(latents.shape))]
        + [whole(a) for a in (wq, wk, wv, wo) + tuple(vectors)],
        [(s, d, by_image(s)) for s, d in outs],
        prefetch=(buckets,),
        flops=images * keys_all * width * inner * 5,
    )


def middle_body(
    core_ref, latent_ref, own_ref, far_ref, gain_ref, bias_ref,
    mid_ref, low_ref, send_ref, first_ref, second_ref,
):
    middle = latent_ref[...].astype(SINGLE) + (own_ref[...] + far_ref[...])
    mid_ref[...] = middle
    _, center, inverse = moments(middle)
    low = (center * inverse * gain_ref[...] + bias_ref[...]).astype(HALF)
    low_ref[...] = low
    half = low.shape[0] // 2
    for which in range(2):

        @pl.when(core_ref[0] == which)
        def _():
            send = low[which * half : (which + 1) * half].astype(SINGLE)
            send_ref[...] = send
            first_ref[...] = send[: first_ref.shape[0]]
            second_ref[...] = send[first_ref.shape[0] :]


def feed_body(low_ref, cot_ref, up_ref, down_ref, hidden_ref, grad_ref, part_ref, out_ref):
    half = up_ref.shape[1] // 2
    total, result = None, None
    for at in range(2):
        cols = slice(at * half, (at + 1) * half)
        value, slope = exact_gelu(dot(low_ref[...], up_ref[:, cols]))
        value = value.astype(HALF)
        hidden_ref[:, cols] = value
        grad = (slope * dot(cot_ref[...], down_ref[cols], 1, 1)).astype(HALF)
        grad_ref[:, cols] = grad
        piece = dot(grad, up_ref[:, cols], 1, 1)
        total = piece if total is None else total + piece
        piece = dot(value, down_ref[cols])
        result = piece if result is None else result + piece

    @pl.when(pl.program_id(0) == 0)
    def _():
        part_ref[...] = total
        out_ref[...] = result

    @pl.when(pl.program_id(0) > 0)
    def _():
        part_ref[...] += total
        out_ref[...] += result


def feed(low, cot, up, down):
    rows, width = low.shape
    hidden = up.shape[1]
    block = 512
    return call(
        feed_body,
        "feed",
        (hidden // block,),
        [
            whole(low),
            whole(cot),
            (up, pl.BlockSpec((width, block), lambda at: (0, at))),
            (down, pl.BlockSpec((block, width), lambda at: (at, 0))),
        ],
        [
            ((rows, hidden), HALF, pl.BlockSpec((rows, block), lambda at: (0, at))),
            ((rows, hidden), HALF, pl.BlockSpec((rows, block), lambda at: (0, at))),
            ((rows, width), SINGLE, pl.BlockSpec((rows, width), lambda at: (0, 0))),
            ((rows, width), SINGLE, pl.BlockSpec((rows, width), lambda at: (0, 0))),
        ],
        flops=8 * rows * width * hidden,
    )


def put_shares(value, place_ref, leave_ref, keep_ref):
    held, share = leave_ref.shape[:2]
    per = value.shape[0] // share
    for at in range(per):
        rows = value[at * share : (at + 1) * share]
        spot = place_ref[pl.program_id(0) * per + at]

        @pl.when(spot < held)
        def _():
            leave_ref[spot] = rows

        @pl.when(spot >= held)
        def _():
            keep_ref[spot - held] = rows


def down_side_body(member_ref, place_ref, *refs, counts):
    feeds, cots = refs[: counts[0]], refs[counts[0] : sum(counts)]
    up_ref, low_ref, cot_ref, own_ref = refs[sum(counts) :][:4]
    leave_ref, keep_ref, fl_ref, cl_ref, slope_ref = refs[sum(counts) + 4 :][:5]
    hid_ref, fbuf, cbuf, sems = refs[sum(counts) + 9 :]
    far = fbuf.shape[0]
    third = far // 3

    @pl.when(pl.program_id(0) == 0)
    def _():
        started = []
        for side, (arrays, buffer) in enumerate(((feeds, fbuf), (cots, cbuf))):
            first = 0
            for at, array in enumerate(arrays):
                count = array.shape[0]
                rows = pl.ds(first, count)
                copy = pltpu.make_async_copy(array, buffer.at[rows], sems.at[side, at])
                copy.start()
                started.append((copy, side, first))
                first += count
        for at in range(3):
            here = slice(at * third, (at + 1) * third)
            for copy, side, first in started:
                if side == 0 and here.start <= first < here.stop:
                    copy.wait()
            low = fbuf[here].astype(HALF)
            fl_ref[here] = low
            value, slope = exact_gelu(dot(low, up_ref[...]))
            hid_ref[here] = value.astype(HALF)
            slope_ref[here] = slope
        fl_ref[far:] = low_ref[...]
        hid_ref[far:] = own_ref[...]
        for copy, side, first in started:
            if side == 1:
                copy.wait()
        cl_ref[:far] = cbuf[...].astype(HALF)
        cl_ref[far:] = cot_ref[...]

    cols = pl.ds(pl.multiple_of(pl.program_id(0) * WIDE, WIDE), WIDE)
    put_shares(dot(cl_ref[:, cols], hid_ref[...], 0, 0), place_ref, leave_ref, keep_ref)


def down_side(member, place, feeds, cots, up, low, cot, hidden, devices):
    rows, width = low.shape
    far = 3 * rows
    total = far + rows
    counts = (len(feeds), len(cots))
    piece = up.shape[1] // GROUP
    every = pl.BlockSpec(memory_space=pl.ANY)
    shape = (devices // 2, width // devices, piece)
    fixed = [
        (shape, SINGLE), (shape, SINGLE), ((total, width), HALF), ((total, width), HALF),
        ((far, piece), SINGLE),
    ]
    return call(
        functools.partial(down_side_body, counts=counts),
        "down_side",
        (width // WIDE,),
        [(a, every) for a in feeds + cots]
        + [
            (up, pl.BlockSpec((width, piece), lambda at, m, p: (0, m[0]))),
            whole(low),
            whole(cot),
            (hidden, pl.BlockSpec((rows, piece), lambda at, m, p: (0, m[0]))),
        ],
        [(s, d, whole(jax.ShapeDtypeStruct(s, d))[1]) for s, d in fixed],
        scratch=[
            pltpu.VMEM((total, piece), HALF),
            pltpu.VMEM((far, width), SINGLE),
            pltpu.VMEM((far, width), SINGLE),
            pltpu.SemaphoreType.DMA((2, max(counts))),
        ],
        prefetch=(member, place),
    )


def up_side_body(
    member_ref, place_ref, fl_ref, cl_ref, slope_ref, down_ref, own_ref, leave_ref, keep_ref, gp_ref
):
    far = slope_ref.shape[0]
    third = far // 3

    @pl.when(pl.program_id(0) == 0)
    def _():
        for at in range(3):
            here = slice(at * third, (at + 1) * third)
            grad = slope_ref[here] * dot(cl_ref[here], down_ref[...], 1, 1)
            gp_ref[here] = grad.astype(HALF)
        gp_ref[far:] = own_ref[...]

    put_shares(dot(fl_ref[...], gp_ref[...], 0, 0), place_ref, leave_ref, keep_ref)


def up_side(member, place, fl, cl, slope, down, grad, devices):
    total, width = fl.shape
    far, piece = slope.shape
    rows = total - far
    shape = (devices // 2, width // devices, piece)
    spec = pl.BlockSpec(shape, lambda at, m, p: (0, 0, 0))
    return call(
        up_side_body,
        "up_side",
        (width // WIDE,),
        [
            (fl, pl.BlockSpec((total, WIDE), lambda at, m, p: (0, at))),
            (cl, pl.BlockSpec((far, width), lambda at, m, p: (0, 0))),
            whole(slope),
            (down, pl.BlockSpec((piece, width), lambda at, m, p: (m[0], 0))),
            (grad, pl.BlockSpec((rows, piece), lambda at, m, p: (0, m[0]))),
        ],
        [(shape, SINGLE, spec), (shape, SINGLE, spec)],
        scratch=[pltpu.VMEM((total, piece), HALF)],
        prefetch=(member, place),
    )


def back_body(
    mid_ref, own_ref, far_ref, cot_ref, gain_ref, wo_ref, q_ref, k_ref, v_ref, p_ref,
    gm_ref, gb_ref, gkv_ref, gkv_send_ref, gq_ref, gq_send_ref, vec_ref,
):
    inner = wo_ref.shape[0]
    heads = inner // HEAD
    upstream = own_ref[...] + far_ref[...]
    _, center, inverse = moments(mid_ref[...])
    moved, product = norm_back(upstream, center * inverse, inverse, gain_ref[...])
    grad_middle = cot_ref[...].astype(SINGLE) + moved
    gm_ref[...] = grad_middle
    branch = grad_middle.astype(HALF)
    gb_ref[...] = branch
    sums = (row_sums(product), row_sums(upstream))

    @pl.when(pl.program_id(0) == 0)
    def _():
        vec_ref[0], vec_ref[1] = sums

    @pl.when(pl.program_id(0) > 0)
    def _():
        vec_ref[0] += sums[0]
        vec_ref[1] += sums[1]

    attended = head_rows(dot(branch, wo_ref[...], 1, 1).astype(HALF), heads)
    query = head_rows(q_ref[0] * HALF(HEAD**-0.5), heads)
    probs = p_ref[0]
    grad_probs = dot(attended, v_ref[0], 1, 1)
    inside = jnp.sum(probs * grad_probs, -1, keepdims=True)
    scores = (probs * (grad_probs - inside)).astype(HALF)
    grad_query = (head_merge(dot(scores, k_ref[0]), heads) * HEAD**-0.5).astype(HALF)
    gq_ref[0] = grad_query
    gq_send_ref[0] = grad_query.astype(SINGLE)
    grad_key = dot(scores, query, 0, 0).astype(HALF)
    gkv_ref[0, :, :inner] = grad_key
    gkv_send_ref[0, :, :inner] = grad_key.astype(SINGLE)
    grad_value = dot(probs.astype(HALF), attended, 0, 0).astype(HALF)
    gkv_ref[0, :, inner:] = grad_value
    gkv_send_ref[0, :, inner:] = grad_value.astype(SINGLE)


def back(middle, own, far, cot, gain, wo, q, k, v, p):
    images, latent_rows, inner = q.shape
    keys_all = k.shape[1]
    rows, width = middle.shape
    line = by_rows(latent_rows, width)
    outs = [
        ((rows, width), SINGLE, line),
        ((rows, width), HALF, line),
        ((images, keys_all, 2 * inner), HALF, by_image((images, keys_all, 2 * inner))),
        ((images, keys_all, 2 * inner), SINGLE, by_image((images, keys_all, 2 * inner))),
        ((images, latent_rows, inner), HALF, by_image(q.shape)),
        ((images, latent_rows, inner), SINGLE, by_image(q.shape)),
        ((2, 8, width), SINGLE, pl.BlockSpec((2, 8, width), lambda at: (0, 0, 0))),
    ]
    return call(
        back_body,
        "back",
        (images,),
        [(a, line) for a in (middle, own, far, cot)]
        + [whole(gain), whole(wo)]
        + [(a, by_image(a.shape)) for a in (q, k, v, p)],
        outs,
        flops=images * 10 * q.shape[1] * 4 * keys_all * inner,
    )


def small_grad_body(place_ref, kv_ref, gb_ref, gkv_ref, gq_ref, att_ref, send_ref, keep_ref, *, images, patches):
    share = send_ref.shape[1]
    inner = att_ref.shape[1]
    held = send_ref.shape[0]
    per = WIDE // share
    keys_all = kv_ref.shape[0] // images
    latent = jnp.concatenate(
        [kv_ref[i * keys_all + patches : (i + 1) * keys_all] for i in range(images)], 0
    )
    pair = dot(kv_ref[...], gkv_ref[...], 0, 0)
    query = dot(latent, gq_ref[...], 0, 0)
    output = dot(gb_ref[...], att_ref[...], 0, 0)
    for at in range(per):
        rows = slice(at * share, (at + 1) * share)
        spot = place_ref[pl.program_id(0) * per + at]

        @pl.when(spot < held)
        def _():
            send_ref[spot, :, : 2 * inner] = pair[rows]
            send_ref[spot, :, 2 * inner : 3 * inner] = query[rows]
            send_ref[spot, :, 3 * inner :] = output[rows]

        @pl.when(spot >= held)
        def _():
            keep_ref[spot - held, :, : 2 * inner] = pair[rows]
            keep_ref[spot - held, :, 2 * inner : 3 * inner] = query[rows]
            keep_ref[spot - held, :, 3 * inner :] = output[rows]


def small_grad(place, kv, gb, gkv, gq, att, devices, images, patches):
    rows, width = kv.shape
    inner = att.shape[1]
    shape = (devices // 2, width // devices, 4 * inner)
    spec = pl.BlockSpec(shape, lambda at, p: (0, 0, 0))
    return call(
        functools.partial(small_grad_body, images=images, patches=patches),
        "small_grad",
        (width // WIDE,),
        [
            (kv, pl.BlockSpec((rows, WIDE), lambda at, p: (0, at))),
            (gb, pl.BlockSpec((gb.shape[0], WIDE), lambda at, p: (0, at))),
        ]
        + [whole(a) for a in (gkv, gq, att)],
        [(shape, SINGLE, spec), (shape, SINGLE, spec)],
        prefetch=(place,),
        flops=4 * rows * width * inner,
    )


def inputs_body(
    gkv_ref, gkv_far_ref, gq_ref, gq_far_ref, media_ref, mean_ref, inv_ref, latent_ref, gm_ref,
    wq_ref, wk_ref, wv_ref, far_ref, mg_ref, lg_ref, before_ref,
    out_ref, late_ref, sums_ref, heads_ref, query_ref, vec_ref,
):
    inner = wq_ref.shape[1]
    patches = media_ref.shape[1]

    @pl.when(pl.program_id(0) == 0)
    def _():
        heads_ref[:, :inner] = wk_ref[...]
        heads_ref[:, inner : 2 * inner] = wv_ref[...]
        heads_ref[:, 2 * inner :] = far_ref[:, inner:].astype(HALF)
        query_ref[:, :inner] = wq_ref[...]
        query_ref[:, inner:] = far_ref[:, :inner].astype(HALF)
        vec_ref[...] = jnp.zeros_like(vec_ref)

    chunk = patches // 3
    for at in range(3):
        rows = slice(at * chunk, (at + 1) * chunk)
        left = jnp.concatenate([gkv_ref[0, rows], gkv_far_ref[0, rows].astype(HALF)], 1)
        upstream = dot(left, heads_ref[...], 1, 1)
        inverse = inv_ref[0, rows]
        normed = (media_ref[0, rows].astype(SINGLE) - mean_ref[0, rows]) * inverse
        moved, product = norm_back(upstream, normed, inverse, mg_ref[...])
        out_ref[0, rows] = moved.astype(HALF)
        vec_ref[0] += row_sums(product)
        vec_ref[1] += row_sums(upstream)
    left = jnp.concatenate([gkv_ref[0, patches:], gkv_far_ref[0, patches:].astype(HALF)], 1)
    upstream = dot(left, heads_ref[...], 1, 1)
    left = jnp.concatenate([gq_ref[0], gq_far_ref[0].astype(HALF)], 1)
    upstream += dot(left, query_ref[...], 1, 1)
    _, center, inverse = moments(latent_ref[0].astype(SINGLE))
    moved, product = norm_back(upstream, center * inverse, inverse, lg_ref[...])
    late_ref[0] = (gm_ref[0] + moved).astype(HALF)
    vec_ref[2] += row_sums(product)
    vec_ref[3] += row_sums(upstream)

    @pl.when(pl.program_id(0) == pl.num_programs(0) - 1)
    def _():
        for at in range(4):
            sums_ref[at : at + 1] = jnp.sum(vec_ref[at], 0, keepdims=True)
        if len(before_ref.shape) == 2:
            sums_ref[:4] += before_ref[:4]
            sums_ref[4:] = before_ref[4:]
        else:
            for at in range(2):
                sums_ref[at + 4 : at + 5] = jnp.sum(before_ref[at], 0, keepdims=True)
            sums_ref[6:] = jnp.zeros_like(sums_ref[6:])


def inputs_back(first, count, held, gkv, gkv_far, gq, gq_far, media, mean, inv, latents, gm, weights):
    images, patches, width = media.shape
    inner = weights[0].shape[1]
    vec = (8, width)

    def image(array):
        rest = (0,) * (array.ndim - 1)
        return pl.BlockSpec((1,) + array.shape[1:], lambda at: (at + first,) + rest)

    arrays = (gkv, gkv_far, gq, gq_far, media, mean, inv, latents, gm)
    ins = [(a, image(a)) for a in arrays] + [whole(a) for a in weights]
    ins += [(a, pl.BlockSpec(memory_space=pl.ANY)) for a in held]
    body = inputs_body
    if held:
        def body(*refs):
            inputs_body(*refs[: len(arrays) + len(weights)], *refs[len(ins) :])

    return call(
        body,
        "inputs_back",
        (count,),
        ins,
        [
            (media.shape, HALF, image(media)),
            (latents.shape, HALF, image(latents)),
            (vec, SINGLE, pl.BlockSpec(vec, lambda at: (0, 0))),
        ],
        scratch=[
            pltpu.VMEM((width, 4 * inner), HALF),
            pltpu.VMEM((width, 2 * inner), HALF),
            pltpu.VMEM((4, 8, width), SINGLE),
        ],
        flops=8 * count * patches * width * inner,
        aliases={len(ins) - len(held) + i: i for i in range(len(held))},
    )


def place_body(member_ref, *refs):
    blocks, out_ref = refs[:GROUP], refs[GROUP]
    piece = blocks[0].shape[1]
    for step in range(GROUP):
        spot = member_ref[0] ^ step
        out_ref[:, pl.ds(pl.multiple_of(spot * piece, piece), piece)] = blocks[step][...]


def place_pieces(member, blocks):
    share, piece = blocks[0].shape
    shape = (share, piece * GROUP)
    return call(
        place_body,
        "place_pieces",
        (1,),
        [whole(b) for b in blocks],
        [(shape, SINGLE, pl.BlockSpec(shape, lambda at, m: (0, 0)))],
        prefetch=(member,),
    )[0]


def after(array, *others):
    return lax.optimization_barrier((array,) + others)[0]


def plan(bits):
    if bits == 4:
        return (0, 3), ([1, 2], [2, 1]), ([0, 1, 2, 3], [1, 0, 3, 2])
    top = bits - 1
    rest = list(range(2, top - 1))
    wide_ = ([top, top - 1] + rest, [top - 1, top] + rest)
    return (0, 1), wide_, (list(range(bits)), [1, 0] + list(range(2, bits)))


class Links:
    def __init__(self, devices):
        self.devices = devices
        self.bits = devices.bit_length() - 1
        self.row = lax.axis_index("dp")
        self.core = lax.axis_index("tensor")

    def swap(self, array):
        return lax.ppermute(array, "tensor", [(0, 1), (1, 0)])

    def send(self, array, step_zero, step_one):
        pairs = []
        for row in range(self.devices):
            pairs.append((2 * row, 2 * (row ^ step_zero)))
            pairs.append((2 * row + 1, 2 * (row ^ step_one) + 1))
        return lax.ppermute(array, ("dp", "tensor"), pairs)

    def bit(self, which):
        return (self.row >> which) & 1

    def places(self, orders, group):
        apart = jnp.arange(self.devices, dtype=jnp.int32) ^ self.row
        found = []
        for order in orders:
            spot = jnp.zeros_like(apart)
            for which in order:
                spot = 2 * spot + 1 - ((apart >> which) & 1)
            for which in reversed(group):
                spot = 2 * spot + ((apart >> which) & 1)
            found.append(spot)
        return jnp.where(self.core == 0, found[0], found[1])

class Halving:
    def __init__(self, links, leave, keep, orders):
        self.links, self.keep, self.orders = links, keep, orders
        self.left = len(orders[0])
        self.send(leave)

    def send(self, leave):
        zero, one = self.orders
        self.come = self.links.send(leave, 1 << zero[-self.left], 1 << one[-self.left])

    def advance(self, *done):
        keep = after(self.keep, *done)
        self.left -= 1
        if not self.left:
            return keep + self.come
        half = keep.shape[0] // 2
        leave, self.keep = keep[:half] + self.come[:half], keep[half:] + self.come[half:]
        self.send(leave)
        return leave


class Total:
    def __init__(self, links, array, order):
        self.links, self.array, self.order = links, array, list(order)
        self.send()

    def send(self):
        hop = 1 << self.order.pop(0)
        self.come = self.links.send(self.array, hop, hop)

    def advance(self, *done):
        self.array = after(self.array, *done) + self.come
        if self.order:
            self.send()
        return self.array


def local(
    media, buckets, latents, cotangent, query_weight, key_weight, value_weight, output_weight,
    up_weight, down_weight, media_gain, media_bias, latent_gain, latent_bias, feed_gain, feed_bias,
    devices,
):
    links = Links(devices)
    images, patches, width = media.shape
    latent_rows = latents.shape[1]
    rows = images * latent_rows
    inner = query_weight.shape[1]
    keys_all = patches + latent_rows
    share = width // devices
    vectors = [v.reshape(1, width) for v in (media_gain, media_bias, latent_gain, latent_bias)]
    gain, bias = feed_gain.reshape(1, width), feed_bias.reshape(1, width)
    core = links.core.reshape(1)
    bits = links.bits
    group, wide_orders, small_orders = plan(bits)
    near_bit, far_bit = 1 << group[0], 1 << group[1]
    member = (links.bit(group[0]) + 2 * links.bit(group[1])).reshape(1)

    cot = cotangent.reshape(rows, width)
    half = rows // 2
    cot_own = lax.dynamic_slice_in_dim(cot, links.core * half, half, 0).astype(SINGLE)
    cut = half // 8 * 5
    cot_far_a = links.send(cot_own[:cut], far_bit, far_bit)
    cot_near = links.send(cot_own, near_bit, near_bit)
    kv, q, k, v, probs, attended, branch, mean, inv = attend(
        buckets, media, latents, query_weight, key_weight, value_weight, output_weight, vectors
    )
    branch, cot_own, cot_near, cot_far_a = lax.optimization_barrier(
        (branch, cot_own, cot_near, cot_far_a)
    )
    branch = branch.reshape(rows, width)
    cot_far_b = links.send(cot_own[cut:], far_bit, far_bit)
    cot_both_a = links.send(cot_far_a, near_bit, near_bit)
    cot_near_other = links.swap(cot_near)
    branch_far = links.swap(branch)
    weights_send = jnp.concatenate(
        [after(query_weight, branch), key_weight, value_weight], 1
    ).astype(SINGLE)
    middle, low, low_send, low_first, low_second = call(
        middle_body,
        "middle",
        (1,),
        [
            whole(a)
            for a in (
                latents.reshape(rows, width),
                after(branch, weights_send),
                branch_far,
                gain,
                bias,
            )
        ],
        [
            ((rows, width), SINGLE, pl.BlockSpec((rows, width), lambda at, c: (0, 0))),
            ((rows, width), HALF, pl.BlockSpec((rows, width), lambda at, c: (0, 0))),
            ((half, width), SINGLE, pl.BlockSpec((half, width), lambda at, c: (0, 0))),
        ]
        + [((r, width), SINGLE, pl.BlockSpec((r, width), lambda at, c: (0, 0))) for r in (half - cut, cut)],
        prefetch=(core,),
    )
    weights_far = links.swap(weights_send)
    low, low_send, low_first, cot_far_a, cot_far_b, cot_both_a = lax.optimization_barrier(
        (low, low_send, low_first, cot_far_a, cot_far_b, cot_both_a, cot_near_other, weights_far)
    )[:6]
    low_far_a = links.send(low_first, far_bit, far_bit)
    cot_both_b = links.send(cot_far_b, near_bit, near_bit)
    cot_far_a_other, cot_both_a_other = links.swap(cot_far_a), links.swap(cot_both_a)
    cot_far_b_other = links.swap(cot_far_b)
    hidden, grad_pre, part, feed_out = feed(low, cot, up_weight, down_weight)
    part, low_far_a, low_send, low_second, cot_both_b = lax.optimization_barrier(
        (
            part, low_far_a, low_send, low_second, cot_both_b,
            cot_far_a_other, cot_both_a_other, cot_far_b_other,
        )
    )[:5]
    part_far = links.swap(part)
    low_far_b = links.send(low_second, far_bit, far_bit)
    low_near = links.send(low_send, near_bit, near_bit)
    low_both_a = links.send(low_far_a, near_bit, near_bit)
    low_far_a_other = links.swap(low_far_a)
    cot_both_b_other = links.swap(cot_both_b)
    grad_middle, grad_branch, gkv, gkv_send, gq, gq_send, feed_vec = back(
        middle, part, part_far, cot, gain, output_weight, q, k, v, probs
    )
    grad_branch, gkv_send, low_near, low_far_b, low_both_a = lax.optimization_barrier(
        (
            grad_branch, gkv_send, low_near, low_far_b, low_both_a,
            low_far_a_other, cot_both_b_other,
        )
    )[:5]
    low_both_b = links.send(low_far_b, near_bit, near_bit)
    gkv_far = links.swap(gkv_send)
    low_near_other, low_far_b_other = links.swap(low_near), links.swap(low_far_b)
    low_both_a_other = links.swap(low_both_a)
    small_leave, small_keep = small_grad(
        links.places(small_orders, ()),
        kv.reshape(images * keys_all, width),
        grad_branch,
        gkv.reshape(images * keys_all, 2 * inner),
        gq.reshape(rows, inner),
        attended.reshape(rows, inner),
        devices,
        images,
        patches,
    )
    small_leave, low_both_b, gq_send, feed_out = lax.optimization_barrier(
        (
            small_leave, low_both_b, gq_send, feed_out,
            gkv_far, low_near_other, low_far_b_other, low_both_a_other,
        )
    )[:4]
    low_both_b_other = links.swap(low_both_b)
    small = Halving(links, small_leave, small_keep, small_orders)
    gq_far = links.swap(gq_send)
    feed_far = links.swap(feed_out)
    place = links.places(wide_orders, group)
    down_leave, down_keep, fl, cl, slope = down_side(
        member,
        place,
        [
            low_near, low_near_other, low_far_a, low_far_b, low_far_a_other, low_far_b_other,
            low_both_a, low_both_b, low_both_a_other, low_both_b_other,
        ],
        [
            cot_near, cot_near_other, cot_far_a, cot_far_b, cot_far_a_other, cot_far_b_other,
            cot_both_a, cot_both_b, cot_both_a_other, cot_both_b_other,
        ],
        up_weight,
        low,
        cot,
        hidden,
        devices,
    )
    down = Halving(links, down_leave, down_keep, wide_orders)
    inputs = (gkv_far, gq, gq_far, media, mean, inv, latents)
    inputs += (grad_middle.reshape(images, latent_rows, width),)
    weights = (query_weight, key_weight, value_weight, weights_far, vectors[0], vectors[2])
    part = images // 2
    early = inputs_back(0, part, (), after(gkv, down_leave), *inputs, weights + (feed_vec,))
    done = down.advance(small.advance(early[2], feed_far))
    up_leave, up_keep = up_side(
        member, place, fl, cl, slope, down_weight, after(grad_pre, done), devices
    )

    hops = [near_bit * (at & 1) + far_bit * (at >> 1) for at in range(GROUP)]

    def pieces(mixed):
        return [mixed[0]] + [links.send(mixed[at], hops[at], hops[at]) for at in range(1, GROUP)]

    done = up_leave
    while down.left > 1:
        done = down.advance(done)
    mixed = down.advance(done)
    up = Halving(links, after(up_leave, mixed), up_keep, wide_orders)
    down_pieces = pieces(mixed)
    grad_media, grad_latents, vec = inputs_back(
        part, images - part, early[:2], after(gkv, mixed), *inputs, weights + (early[2],)
    )
    down_pieces = list(lax.optimization_barrier(tuple(down_pieces) + (vec,)))
    done = vec = down_pieces.pop()
    while up.left > 1:
        done = up.advance(done)
    vec = Total(links, after(vec, done), [group[1], group[0]] + wide_orders[0])
    done = small.advance(vec.array)
    done = result = (after(middle, done) + (feed_out + feed_far)).astype(HALF)
    done = vec.advance(done)
    mixed = up.advance(done)
    up_pieces = pieces(mixed)
    done = vec.advance(mixed, up_pieces[1])
    down_pieces[0] = after(down_pieces[0], done)
    done = grad_down = place_pieces(member, down_pieces)
    while vec.order:
        done = vec.advance(done)
    while small.left > 1:
        done = small.advance(done, up_pieces[2])
    vec = vec.advance(done, up_pieces[3])
    vec = lax.dynamic_slice_in_dim(vec, links.row * share, share, 1)
    up_pieces[0] = after(up_pieces[0], vec)
    grad_up = place_pieces(member, up_pieces)
    small = small.advance(grad_up)[0]
    return (
        result.reshape(latents.shape),
        grad_media,
        grad_latents,
        small[:, 2 * inner : 3 * inner],
        small[:, :inner],
        small[:, inner : 2 * inner],
        small[:, 3 * inner :].T,
        grad_up,
        grad_down.T,
    ) + tuple(vec[at] for at in range(6))


def solution(mesh):
    devices = mesh.shape["dp"]
    images = P("dp", None, None)
    columns = P(None, "tensor")
    lines = P("tensor", None)

    def body(*args):
        return local(*args, devices=devices)

    return jax.shard_map(
        body,
        mesh=mesh,
        in_specs=(images, P("dp"), images, images)
        + (columns, columns, columns, lines, columns, lines)
        + (P(),) * 6,
        out_specs=(images,) * 3
        + (P("dp", "tensor"),) * 3
        + (P("tensor", "dp"), P("dp", "tensor"), P("tensor", "dp"))
        + (P("dp"),) * 6,
        check_vma=False,
    )
```

```python
import functools

import jax
import jax.numpy as jnp
from jax import lax
from jax.experimental import pallas as pl
from jax.experimental.pallas import tpu as pltpu
from jax.sharding import PartitionSpec as P

HEAD = 64
PATCH = 576
SHORT = 256
GROUP = 4
LANES = 128
WIDE = 256
EPSILON = 1e-05
SINGLE = jnp.float32
HALF = jnp.bfloat16


def dot(left, right, left_axis=1, right_axis=0):
    return lax.dot_general(
        left, right, (((left_axis,), (right_axis,)), ((), ())), preferred_element_type=SINGLE
    )


def moments(values):
    mean = jnp.mean(values, -1, keepdims=True)
    center = values - mean
    inverse = lax.rsqrt(jnp.mean(center * center, -1, keepdims=True) + EPSILON)
    return mean, center, inverse


def norm_back(upstream, normed, inverse, gain):
    product = upstream * normed
    scaled = upstream * gain
    shift = jnp.mean(scaled, -1, keepdims=True)
    slope = jnp.mean(product * gain, -1, keepdims=True)
    return inverse * (scaled - shift - normed * slope), product


def row_sums(values):
    count, width = values.shape
    return jnp.sum(values.reshape(count // 8, 8, width), axis=0)


def head_rows(array, heads):
    column = lax.broadcasted_iota(jnp.int32, array.shape, 1) // HEAD
    return jnp.concatenate([jnp.where(column == h, array, 0) for h in range(heads)], 0)


def head_merge(blocks, heads):
    rows = blocks.shape[0] // heads
    total = None
    for h in range(heads):
        part = blocks[h * rows : (h + 1) * rows]
        column = lax.broadcasted_iota(jnp.int32, part.shape, 1) // HEAD
        part = jnp.where(column == h, part, 0)
        total = part if total is None else total + part
    return total


def exact_gelu(values):
    below = 0.5 * (1.0 + lax.erf(values * (0.5**0.5)))
    density = jnp.exp(values * values * -0.5) * 0.3989422804014327
    return values * below, below + values * density


def call(body, name, grid, ins, outs, scratch=(), prefetch=(), flops=0, aliases=None):
    moved = sum(a.size * a.dtype.itemsize for a, _ in ins)
    shapes = [jax.ShapeDtypeStruct(s, d) for s, d, _ in outs]
    moved += sum(s.size * s.dtype.itemsize for s in shapes)
    return pl.pallas_call(
        body,
        out_shape=shapes,
        grid_spec=pltpu.PrefetchScalarGridSpec(
            num_scalar_prefetch=len(prefetch),
            grid=grid,
            in_specs=[s for _, s in ins],
            out_specs=[s for _, _, s in outs],
            scratch_shapes=list(scratch),
        ),
        cost_estimate=pl.CostEstimate(flops=flops, bytes_accessed=moved, transcendentals=0),
        input_output_aliases=aliases or {},
        name=name,
    )(*prefetch, *[a for a, _ in ins])


def whole(array):
    zeros = (0,) * array.ndim
    return array, pl.BlockSpec(array.shape, lambda *at: zeros)


def by_image(shape):
    rest = (0,) * (len(shape) - 1)
    return pl.BlockSpec((1,) + tuple(shape[1:]), lambda at, *_: (at,) + rest)


def by_rows(rows, width):
    return pl.BlockSpec((rows, width), lambda at, *_: (at, 0))


def attend_body(
    buckets_ref, media_ref, latent_ref, wq_ref, wk_ref, wv_ref, wo_ref,
    mg_ref, mb_ref, lg_ref, lb_ref,
    kv_ref, q_ref, k_ref, v_ref, p_ref, att_ref, branch_ref, mean_ref, inv_ref,
):
    patches = media_ref.shape[1]
    latent_rows = latent_ref.shape[1]
    inner = wq_ref.shape[1]
    heads = inner // HEAD
    chunk = patches // 3
    for at in range(3):
        rows = slice(at * chunk, (at + 1) * chunk)
        mean, center, inverse = moments(media_ref[0, rows].astype(SINGLE))
        mean_ref[0, rows] = mean
        inv_ref[0, rows] = inverse
        low = (center * inverse * mg_ref[...] + mb_ref[...]).astype(HALF)
        kv_ref[0, rows] = low
        k_ref[0, rows] = dot(low, wk_ref[...]).astype(HALF)
        v_ref[0, rows] = dot(low, wv_ref[...]).astype(HALF)
    rows = slice(patches, patches + latent_rows)
    _, center, inverse = moments(latent_ref[0].astype(SINGLE))
    low = (center * inverse * lg_ref[...] + lb_ref[...]).astype(HALF)
    kv_ref[0, rows] = low
    k_ref[0, rows] = dot(low, wk_ref[...]).astype(HALF)
    v_ref[0, rows] = dot(low, wv_ref[...]).astype(HALF)
    query = dot(low, wq_ref[...]).astype(HALF)
    q_ref[0] = query
    spread = head_rows(query * HALF(HEAD**-0.5), heads)
    scores = dot(spread, k_ref[0], 1, 1)
    count = SHORT + (PATCH - SHORT) * buckets_ref[pl.program_id(0)]
    column = lax.broadcasted_iota(jnp.int32, scores.shape, 1)
    scores = jnp.where((column < count) | (column >= patches), scores, -1e30)
    shifted = jnp.exp(scores - jnp.max(scores, -1, keepdims=True))
    probs = shifted / jnp.sum(shifted, -1, keepdims=True)
    p_ref[0] = probs
    attended = head_merge(dot(probs.astype(HALF), v_ref[0]), heads).astype(HALF)
    att_ref[0] = attended
    branch_ref[0] = dot(attended, wo_ref[...])


def attend(buckets, media, latents, wq, wk, wv, wo, vectors):
    images, patches, width = media.shape
    latent_rows = latents.shape[1]
    inner = wq.shape[1]
    keys_all = patches + latent_rows
    heads = inner // HEAD
    outs = [
        ((images, keys_all, width), HALF),
        ((images, latent_rows, inner), HALF),
        ((images, keys_all, inner), HALF),
        ((images, keys_all, inner), HALF),
        ((images, heads * latent_rows, keys_all), SINGLE),
        ((images, latent_rows, inner), HALF),
        ((images, latent_rows, width), SINGLE),
        ((images, patches, 1), SINGLE),
        ((images, patches, 1), SINGLE),
    ]
    return call(
        attend_body,
        "attend",
        (images,),
        [(media, by_image(media.shape)), (latents, by_image(latents.shape))]
        + [whole(a) for a in (wq, wk, wv, wo) + tuple(vectors)],
        [(s, d, by_image(s)) for s, d in outs],
        prefetch=(buckets,),
        flops=images * keys_all * width * inner * 5,
    )


def middle_body(
    core_ref, latent_ref, own_ref, far_ref, gain_ref, bias_ref,
    mid_ref, low_ref, send_ref, first_ref, second_ref,
):
    middle = latent_ref[...].astype(SINGLE) + (own_ref[...] + far_ref[...])
    mid_ref[...] = middle
    _, center, inverse = moments(middle)
    low = (center * inverse * gain_ref[...] + bias_ref[...]).astype(HALF)
    low_ref[...] = low
    half = low.shape[0] // 2
    for which in range(2):

        @pl.when(core_ref[0] == which)
        def _():
            send = low[which * half : (which + 1) * half].astype(SINGLE)
            send_ref[...] = send
            first_ref[...] = send[: first_ref.shape[0]]
            second_ref[...] = send[first_ref.shape[0] :]


def feed_body(low_ref, cot_ref, up_ref, down_ref, hidden_ref, grad_ref, part_ref, out_ref):
    half = up_ref.shape[1] // 2
    total, result = None, None
    for at in range(2):
        cols = slice(at * half, (at + 1) * half)
        value, slope = exact_gelu(dot(low_ref[...], up_ref[:, cols]))
        value = value.astype(HALF)
        hidden_ref[:, cols] = value
        grad = (slope * dot(cot_ref[...], down_ref[cols], 1, 1)).astype(HALF)
        grad_ref[:, cols] = grad
        piece = dot(grad, up_ref[:, cols], 1, 1)
        total = piece if total is None else total + piece
        piece = dot(value, down_ref[cols])
        result = piece if result is None else result + piece

    @pl.when(pl.program_id(0) == 0)
    def _():
        part_ref[...] = total
        out_ref[...] = result

    @pl.when(pl.program_id(0) > 0)
    def _():
        part_ref[...] += total
        out_ref[...] += result


def feed(low, cot, up, down):
    rows, width = low.shape
    hidden = up.shape[1]
    block = 512
    return call(
        feed_body,
        "feed",
        (hidden // block,),
        [
            whole(low),
            whole(cot),
            (up, pl.BlockSpec((width, block), lambda at: (0, at))),
            (down, pl.BlockSpec((block, width), lambda at: (at, 0))),
        ],
        [
            ((rows, hidden), HALF, pl.BlockSpec((rows, block), lambda at: (0, at))),
            ((rows, hidden), HALF, pl.BlockSpec((rows, block), lambda at: (0, at))),
            ((rows, width), SINGLE, pl.BlockSpec((rows, width), lambda at: (0, 0))),
            ((rows, width), SINGLE, pl.BlockSpec((rows, width), lambda at: (0, 0))),
        ],
        flops=8 * rows * width * hidden,
    )


def put_shares(value, place_ref, leave_ref, keep_ref):
    held, share = leave_ref.shape[:2]
    per = value.shape[0] // share
    for at in range(per):
        rows = value[at * share : (at + 1) * share]
        spot = place_ref[pl.program_id(0) * per + at]

        @pl.when(spot < held)
        def _():
            leave_ref[spot] = rows

        @pl.when(spot >= held)
        def _():
            keep_ref[spot - held] = rows


def down_side_body(member_ref, place_ref, *refs, counts):
    feeds, cots = refs[: counts[0]], refs[counts[0] : sum(counts)]
    up_ref, low_ref, cot_ref, own_ref = refs[sum(counts) :][:4]
    leave_ref, keep_ref, fl_ref, cl_ref, slope_ref = refs[sum(counts) + 4 :][:5]
    hid_ref, fbuf, cbuf, sems = refs[sum(counts) + 9 :]
    far = fbuf.shape[0]
    third = far // 3

    @pl.when(pl.program_id(0) == 0)
    def _():
        started = []
        for side, (arrays, buffer) in enumerate(((feeds, fbuf), (cots, cbuf))):
            first = 0
            for at, array in enumerate(arrays):
                count = array.shape[0]
                rows = pl.ds(first, count)
                copy = pltpu.make_async_copy(array, buffer.at[rows], sems.at[side, at])
                copy.start()
                started.append((copy, side, first))
                first += count
        for at in range(3):
            here = slice(at * third, (at + 1) * third)
            for copy, side, first in started:
                if side == 0 and here.start <= first < here.stop:
                    copy.wait()
            low = fbuf[here].astype(HALF)
            fl_ref[here] = low
            value, slope = exact_gelu(dot(low, up_ref[...]))
            hid_ref[here] = value.astype(HALF)
            slope_ref[here] = slope
        fl_ref[far:] = low_ref[...]
        hid_ref[far:] = own_ref[...]
        for copy, side, first in started:
            if side == 1:
                copy.wait()
        cl_ref[:far] = cbuf[...].astype(HALF)
        cl_ref[far:] = cot_ref[...]

    cols = pl.ds(pl.multiple_of(pl.program_id(0) * WIDE, WIDE), WIDE)
    put_shares(dot(cl_ref[:, cols], hid_ref[...], 0, 0), place_ref, leave_ref, keep_ref)


def down_side(member, place, feeds, cots, up, low, cot, hidden, devices):
    rows, width = low.shape
    far = 3 * rows
    total = far + rows
    counts = (len(feeds), len(cots))
    piece = up.shape[1] // GROUP
    every = pl.BlockSpec(memory_space=pl.ANY)
    shape = (devices // 2, width // devices, piece)
    fixed = [
        (shape, SINGLE), (shape, SINGLE), ((total, width), HALF), ((total, width), HALF),
        ((far, piece), SINGLE),
    ]
    return call(
        functools.partial(down_side_body, counts=counts),
        "down_side",
        (width // WIDE,),
        [(a, every) for a in feeds + cots]
        + [
            (up, pl.BlockSpec((width, piece), lambda at, m, p: (0, m[0]))),
            whole(low),
            whole(cot),
            (hidden, pl.BlockSpec((rows, piece), lambda at, m, p: (0, m[0]))),
        ],
        [(s, d, whole(jax.ShapeDtypeStruct(s, d))[1]) for s, d in fixed],
        scratch=[
            pltpu.VMEM((total, piece), HALF),
            pltpu.VMEM((far, width), SINGLE),
            pltpu.VMEM((far, width), SINGLE),
            pltpu.SemaphoreType.DMA((2, max(counts))),
        ],
        prefetch=(member, place),
    )


def up_side_body(
    member_ref, place_ref, fl_ref, cl_ref, slope_ref, down_ref, own_ref, leave_ref, keep_ref, gp_ref
):
    far = slope_ref.shape[0]
    third = far // 3

    @pl.when(pl.program_id(0) == 0)
    def _():
        for at in range(3):
            here = slice(at * third, (at + 1) * third)
            grad = slope_ref[here] * dot(cl_ref[here], down_ref[...], 1, 1)
            gp_ref[here] = grad.astype(HALF)
        gp_ref[far:] = own_ref[...]

    put_shares(dot(fl_ref[...], gp_ref[...], 0, 0), place_ref, leave_ref, keep_ref)


def up_side(member, place, fl, cl, slope, down, grad, devices):
    total, width = fl.shape
    far, piece = slope.shape
    rows = total - far
    shape = (devices // 2, width // devices, piece)
    spec = pl.BlockSpec(shape, lambda at, m, p: (0, 0, 0))
    return call(
        up_side_body,
        "up_side",
        (width // WIDE,),
        [
            (fl, pl.BlockSpec((total, WIDE), lambda at, m, p: (0, at))),
            (cl, pl.BlockSpec((far, width), lambda at, m, p: (0, 0))),
            whole(slope),
            (down, pl.BlockSpec((piece, width), lambda at, m, p: (m[0], 0))),
            (grad, pl.BlockSpec((rows, piece), lambda at, m, p: (0, m[0]))),
        ],
        [(shape, SINGLE, spec), (shape, SINGLE, spec)],
        scratch=[pltpu.VMEM((total, piece), HALF)],
        prefetch=(member, place),
    )


def back_body(
    mid_ref, own_ref, far_ref, cot_ref, gain_ref, wo_ref, q_ref, k_ref, v_ref, p_ref,
    gm_ref, gb_ref, gkv_ref, gkv_send_ref, gq_ref, gq_send_ref, vec_ref,
):
    inner = wo_ref.shape[0]
    heads = inner // HEAD
    upstream = own_ref[...] + far_ref[...]
    _, center, inverse = moments(mid_ref[...])
    moved, product = norm_back(upstream, center * inverse, inverse, gain_ref[...])
    grad_middle = cot_ref[...].astype(SINGLE) + moved
    gm_ref[...] = grad_middle
    branch = grad_middle.astype(HALF)
    gb_ref[...] = branch
    sums = (row_sums(product), row_sums(upstream))

    @pl.when(pl.program_id(0) == 0)
    def _():
        vec_ref[0], vec_ref[1] = sums

    @pl.when(pl.program_id(0) > 0)
    def _():
        vec_ref[0] += sums[0]
        vec_ref[1] += sums[1]

    attended = head_rows(dot(branch, wo_ref[...], 1, 1).astype(HALF), heads)
    query = head_rows(q_ref[0] * HALF(HEAD**-0.5), heads)
    probs = p_ref[0]
    grad_probs = dot(attended, v_ref[0], 1, 1)
    inside = jnp.sum(probs * grad_probs, -1, keepdims=True)
    scores = (probs * (grad_probs - inside)).astype(HALF)
    grad_query = (head_merge(dot(scores, k_ref[0]), heads) * HEAD**-0.5).astype(HALF)
    gq_ref[0] = grad_query
    gq_send_ref[0] = grad_query.astype(SINGLE)
    grad_key = dot(scores, query, 0, 0).astype(HALF)
    gkv_ref[0, :, :inner] = grad_key
    gkv_send_ref[0, :, :inner] = grad_key.astype(SINGLE)
    grad_value = dot(probs.astype(HALF), attended, 0, 0).astype(HALF)
    gkv_ref[0, :, inner:] = grad_value
    gkv_send_ref[0, :, inner:] = grad_value.astype(SINGLE)


def back(middle, own, far, cot, gain, wo, q, k, v, p):
    images, latent_rows, inner = q.shape
    keys_all = k.shape[1]
    rows, width = middle.shape
    line = by_rows(latent_rows, width)
    outs = [
        ((rows, width), SINGLE, line),
        ((rows, width), HALF, line),
        ((images, keys_all, 2 * inner), HALF, by_image((images, keys_all, 2 * inner))),
        ((images, keys_all, 2 * inner), SINGLE, by_image((images, keys_all, 2 * inner))),
        ((images, latent_rows, inner), HALF, by_image(q.shape)),
        ((images, latent_rows, inner), SINGLE, by_image(q.shape)),
        ((2, 8, width), SINGLE, pl.BlockSpec((2, 8, width), lambda at: (0, 0, 0))),
    ]
    return call(
        back_body,
        "back",
        (images,),
        [(a, line) for a in (middle, own, far, cot)]
        + [whole(gain), whole(wo)]
        + [(a, by_image(a.shape)) for a in (q, k, v, p)],
        outs,
        flops=images * 10 * q.shape[1] * 4 * keys_all * inner,
    )


def small_grad_body(place_ref, kv_ref, gb_ref, gkv_ref, gq_ref, att_ref, send_ref, keep_ref, *, images, patches):
    share = send_ref.shape[1]
    inner = att_ref.shape[1]
    held = send_ref.shape[0]
    per = WIDE // share
    keys_all = kv_ref.shape[0] // images
    latent = jnp.concatenate(
        [kv_ref[i * keys_all + patches : (i + 1) * keys_all] for i in range(images)], 0
    )
    pair = dot(kv_ref[...], gkv_ref[...], 0, 0)
    query = dot(latent, gq_ref[...], 0, 0)
    output = dot(gb_ref[...], att_ref[...], 0, 0)
    for at in range(per):
        rows = slice(at * share, (at + 1) * share)
        spot = place_ref[pl.program_id(0) * per + at]

        @pl.when(spot < held)
        def _():
            send_ref[spot, :, : 2 * inner] = pair[rows]
            send_ref[spot, :, 2 * inner : 3 * inner] = query[rows]
            send_ref[spot, :, 3 * inner :] = output[rows]

        @pl.when(spot >= held)
        def _():
            keep_ref[spot - held, :, : 2 * inner] = pair[rows]
            keep_ref[spot - held, :, 2 * inner : 3 * inner] = query[rows]
            keep_ref[spot - held, :, 3 * inner :] = output[rows]


def small_grad(place, kv, gb, gkv, gq, att, devices, images, patches):
    rows, width = kv.shape
    inner = att.shape[1]
    shape = (devices // 2, width // devices, 4 * inner)
    spec = pl.BlockSpec(shape, lambda at, p: (0, 0, 0))
    return call(
        functools.partial(small_grad_body, images=images, patches=patches),
        "small_grad",
        (width // WIDE,),
        [
            (kv, pl.BlockSpec((rows, WIDE), lambda at, p: (0, at))),
            (gb, pl.BlockSpec((gb.shape[0], WIDE), lambda at, p: (0, at))),
        ]
        + [whole(a) for a in (gkv, gq, att)],
        [(shape, SINGLE, spec), (shape, SINGLE, spec)],
        prefetch=(place,),
        flops=4 * rows * width * inner,
    )


def inputs_body(
    gkv_ref, gkv_far_ref, gq_ref, gq_far_ref, media_ref, mean_ref, inv_ref, latent_ref, gm_ref,
    wq_ref, wk_ref, wv_ref, far_ref, mg_ref, lg_ref, before_ref,
    out_ref, late_ref, sums_ref, heads_ref, query_ref, vec_ref,
):
    inner = wq_ref.shape[1]
    patches = media_ref.shape[1]

    @pl.when(pl.program_id(0) == 0)
    def _():
        heads_ref[:, :inner] = wk_ref[...]
        heads_ref[:, inner : 2 * inner] = wv_ref[...]
        heads_ref[:, 2 * inner :] = far_ref[:, inner:].astype(HALF)
        query_ref[:, :inner] = wq_ref[...]
        query_ref[:, inner:] = far_ref[:, :inner].astype(HALF)
        vec_ref[...] = jnp.zeros_like(vec_ref)

    chunk = patches // 3
    for at in range(3):
        rows = slice(at * chunk, (at + 1) * chunk)
        left = jnp.concatenate([gkv_ref[0, rows], gkv_far_ref[0, rows].astype(HALF)], 1)
        upstream = dot(left, heads_ref[...], 1, 1)
        inverse = inv_ref[0, rows]
        normed = (media_ref[0, rows].astype(SINGLE) - mean_ref[0, rows]) * inverse
        moved, product = norm_back(upstream, normed, inverse, mg_ref[...])
        out_ref[0, rows] = moved.astype(HALF)
        vec_ref[0] += row_sums(product)
        vec_ref[1] += row_sums(upstream)
    left = jnp.concatenate([gkv_ref[0, patches:], gkv_far_ref[0, patches:].astype(HALF)], 1)
    upstream = dot(left, heads_ref[...], 1, 1)
    left = jnp.concatenate([gq_ref[0], gq_far_ref[0].astype(HALF)], 1)
    upstream += dot(left, query_ref[...], 1, 1)
    _, center, inverse = moments(latent_ref[0].astype(SINGLE))
    moved, product = norm_back(upstream, center * inverse, inverse, lg_ref[...])
    late_ref[0] = (gm_ref[0] + moved).astype(HALF)
    vec_ref[2] += row_sums(product)
    vec_ref[3] += row_sums(upstream)

    @pl.when(pl.program_id(0) == pl.num_programs(0) - 1)
    def _():
        for at in range(4):
            sums_ref[at : at + 1] = jnp.sum(vec_ref[at], 0, keepdims=True)
        if len(before_ref.shape) == 2:
            sums_ref[:4] += before_ref[:4]
            sums_ref[4:] = before_ref[4:]
        else:
            for at in range(2):
                sums_ref[at + 4 : at + 5] = jnp.sum(before_ref[at], 0, keepdims=True)
            sums_ref[6:] = jnp.zeros_like(sums_ref[6:])


def inputs_back(first, count, held, gkv, gkv_far, gq, gq_far, media, mean, inv, latents, gm, weights):
    images, patches, width = media.shape
    inner = weights[0].shape[1]
    vec = (8, width)

    def image(array):
        rest = (0,) * (array.ndim - 1)
        return pl.BlockSpec((1,) + array.shape[1:], lambda at: (at + first,) + rest)

    arrays = (gkv, gkv_far, gq, gq_far, media, mean, inv, latents, gm)
    ins = [(a, image(a)) for a in arrays] + [whole(a) for a in weights]
    ins += [(a, pl.BlockSpec(memory_space=pl.ANY)) for a in held]
    body = inputs_body
    if held:
        def body(*refs):
            inputs_body(*refs[: len(arrays) + len(weights)], *refs[len(ins) :])

    return call(
        body,
        "inputs_back",
        (count,),
        ins,
        [
            (media.shape, HALF, image(media)),
            (latents.shape, HALF, image(latents)),
            (vec, SINGLE, pl.BlockSpec(vec, lambda at: (0, 0))),
        ],
        scratch=[
            pltpu.VMEM((width, 4 * inner), HALF),
            pltpu.VMEM((width, 2 * inner), HALF),
            pltpu.VMEM((4, 8, width), SINGLE),
        ],
        flops=8 * count * patches * width * inner,
        aliases={len(ins) - len(held) + i: i for i in range(len(held))},
    )


def place_body(member_ref, *refs):
    blocks, out_ref = refs[:GROUP], refs[GROUP]
    piece = blocks[0].shape[1]
    for step in range(GROUP):
        spot = member_ref[0] ^ step
        out_ref[:, pl.ds(pl.multiple_of(spot * piece, piece), piece)] = blocks[step][...]


def place_pieces(member, blocks):
    share, piece = blocks[0].shape
    shape = (share, piece * GROUP)
    return call(
        place_body,
        "place_pieces",
        (1,),
        [whole(b) for b in blocks],
        [(shape, SINGLE, pl.BlockSpec(shape, lambda at, m: (0, 0)))],
        prefetch=(member,),
    )[0]


def after(array, *others):
    return lax.optimization_barrier((array,) + others)[0]


def plan(bits):
    if bits == 4:
        return (0, 3), ([1, 2], [2, 1]), ([0, 1, 2, 3], [1, 0, 3, 2])
    top = bits - 1
    rest = list(range(2, top - 1))
    wide_ = ([top, top - 1] + rest, [top - 1, top] + rest)
    return (0, 1), wide_, (list(range(bits)), [1, 0] + list(range(2, bits)))


class Links:
    def __init__(self, devices):
        self.devices = devices
        self.bits = devices.bit_length() - 1
        self.row = lax.axis_index("dp")
        self.core = lax.axis_index("tensor")

    def swap(self, array):
        return lax.ppermute(array, "tensor", [(0, 1), (1, 0)])

    def send(self, array, step_zero, step_one):
        pairs = []
        for row in range(self.devices):
            pairs.append((2 * row, 2 * (row ^ step_zero)))
            pairs.append((2 * row + 1, 2 * (row ^ step_one) + 1))
        return lax.ppermute(array, ("dp", "tensor"), pairs)

    def bit(self, which):
        return (self.row >> which) & 1

    def places(self, orders, group):
        apart = jnp.arange(self.devices, dtype=jnp.int32) ^ self.row
        found = []
        for order in orders:
            spot = jnp.zeros_like(apart)
            for which in order:
                spot = 2 * spot + 1 - ((apart >> which) & 1)
            for which in reversed(group):
                spot = 2 * spot + ((apart >> which) & 1)
            found.append(spot)
        return jnp.where(self.core == 0, found[0], found[1])

class Halving:
    def __init__(self, links, leave, keep, orders):
        self.links, self.keep, self.orders = links, keep, orders
        self.left = len(orders[0])
        self.send(leave)

    def send(self, leave):
        zero, one = self.orders
        self.come = self.links.send(leave, 1 << zero[-self.left], 1 << one[-self.left])

    def advance(self, *done):
        keep = after(self.keep, *done)
        self.left -= 1
        if not self.left:
            return keep + self.come
        half = keep.shape[0] // 2
        leave, self.keep = keep[:half] + self.come[:half], keep[half:] + self.come[half:]
        self.send(leave)
        return leave


class Total:
    def __init__(self, links, array, order):
        self.links, self.array, self.order = links, array, list(order)
        self.send()

    def send(self):
        hop = 1 << self.order.pop(0)
        self.come = self.links.send(self.array, hop, hop)

    def advance(self, *done):
        self.array = after(self.array, *done) + self.come
        if self.order:
            self.send()
        return self.array


def local(
    media, buckets, latents, cotangent, query_weight, key_weight, value_weight, output_weight,
    up_weight, down_weight, media_gain, media_bias, latent_gain, latent_bias, feed_gain, feed_bias,
    devices,
):
    links = Links(devices)
    images, patches, width = media.shape
    latent_rows = latents.shape[1]
    rows = images * latent_rows
    inner = query_weight.shape[1]
    keys_all = patches + latent_rows
    share = width // devices
    vectors = [v.reshape(1, width) for v in (media_gain, media_bias, latent_gain, latent_bias)]
    gain, bias = feed_gain.reshape(1, width), feed_bias.reshape(1, width)
    core = links.core.reshape(1)
    bits = links.bits
    group, wide_orders, small_orders = plan(bits)
    near_bit, far_bit = 1 << group[0], 1 << group[1]
    member = (links.bit(group[0]) + 2 * links.bit(group[1])).reshape(1)

    cot = cotangent.reshape(rows, width)
    half = rows // 2
    cot_own = lax.dynamic_slice_in_dim(cot, links.core * half, half, 0).astype(SINGLE)
    cut = half // 8 * 5
    cot_far_a = links.send(cot_own[:cut], far_bit, far_bit)
    cot_near = links.send(cot_own, near_bit, near_bit)
    kv, q, k, v, probs, attended, branch, mean, inv = attend(
        buckets, media, latents, query_weight, key_weight, value_weight, output_weight, vectors
    )
    branch, cot_own, cot_near, cot_far_a = lax.optimization_barrier(
        (branch, cot_own, cot_near, cot_far_a)
    )
    branch = branch.reshape(rows, width)
    cot_far_b = links.send(cot_own[cut:], far_bit, far_bit)
    cot_both_a = links.send(cot_far_a, near_bit, near_bit)
    cot_near_other = links.swap(cot_near)
    branch_far = links.swap(branch)
    weights_send = jnp.concatenate(
        [after(query_weight, branch), key_weight, value_weight], 1
    ).astype(SINGLE)
    middle, low, low_send, low_first, low_second = call(
        middle_body,
        "middle",
        (1,),
        [
            whole(a)
            for a in (
                latents.reshape(rows, width),
                after(branch, weights_send),
                branch_far,
                gain,
                bias,
            )
        ],
        [
            ((rows, width), SINGLE, pl.BlockSpec((rows, width), lambda at, c: (0, 0))),
            ((rows, width), HALF, pl.BlockSpec((rows, width), lambda at, c: (0, 0))),
            ((half, width), SINGLE, pl.BlockSpec((half, width), lambda at, c: (0, 0))),
        ]
        + [((r, width), SINGLE, pl.BlockSpec((r, width), lambda at, c: (0, 0))) for r in (half - cut, cut)],
        prefetch=(core,),
    )
    weights_far = links.swap(weights_send)
    low, low_send, low_first, cot_far_a, cot_far_b, cot_both_a = lax.optimization_barrier(
        (low, low_send, low_first, cot_far_a, cot_far_b, cot_both_a, cot_near_other, weights_far)
    )[:6]
    low_far_a = links.send(low_first, far_bit, far_bit)
    cot_both_b = links.send(cot_far_b, near_bit, near_bit)
    cot_far_a_other, cot_both_a_other = links.swap(cot_far_a), links.swap(cot_both_a)
    cot_far_b_other = links.swap(cot_far_b)
    hidden, grad_pre, part, feed_out = feed(low, cot, up_weight, down_weight)
    part, low_far_a, low_send, low_second, cot_both_b = lax.optimization_barrier(
        (
            part, low_far_a, low_send, low_second, cot_both_b,
            cot_far_a_other, cot_both_a_other, cot_far_b_other,
        )
    )[:5]
    part_far = links.swap(part)
    low_far_b = links.send(low_second, far_bit, far_bit)
    low_near = links.send(low_send, near_bit, near_bit)
    low_both_a = links.send(low_far_a, near_bit, near_bit)
    low_far_a_other = links.swap(low_far_a)
    cot_both_b_other = links.swap(cot_both_b)
    grad_middle, grad_branch, gkv, gkv_send, gq, gq_send, feed_vec = back(
        middle, part, part_far, cot, gain, output_weight, q, k, v, probs
    )
    grad_branch, gkv_send, low_near, low_far_b, low_both_a = lax.optimization_barrier(
        (
            grad_branch, gkv_send, low_near, low_far_b, low_both_a,
            low_far_a_other, cot_both_b_other,
        )
    )[:5]
    low_both_b = links.send(low_far_b, near_bit, near_bit)
    gkv_far = links.swap(gkv_send)
    low_near_other, low_far_b_other = links.swap(low_near), links.swap(low_far_b)
    low_both_a_other = links.swap(low_both_a)
    small_leave, small_keep = small_grad(
        links.places(small_orders, ()),
        kv.reshape(images * keys_all, width),
        grad_branch,
        gkv.reshape(images * keys_all, 2 * inner),
        gq.reshape(rows, inner),
        attended.reshape(rows, inner),
        devices,
        images,
        patches,
    )
    small_leave, low_both_b, gq_send, feed_out = lax.optimization_barrier(
        (
            small_leave, low_both_b, gq_send, feed_out,
            gkv_far, low_near_other, low_far_b_other, low_both_a_other,
        )
    )[:4]
    low_both_b_other = links.swap(low_both_b)
    small = Halving(links, small_leave, small_keep, small_orders)
    gq_far = links.swap(gq_send)
    feed_far = links.swap(feed_out)
    place = links.places(wide_orders, group)
    down_leave, down_keep, fl, cl, slope = down_side(
        member,
        place,
        [
            low_near, low_near_other, low_far_a, low_far_b, low_far_a_other, low_far_b_other,
            low_both_a, low_both_b, low_both_a_other, low_both_b_other,
        ],
        [
            cot_near, cot_near_other, cot_far_a, cot_far_b, cot_far_a_other, cot_far_b_other,
            cot_both_a, cot_both_b, cot_both_a_other, cot_both_b_other,
        ],
        up_weight,
        low,
        cot,
        hidden,
        devices,
    )
    down = Halving(links, down_leave, down_keep, wide_orders)
    inputs = (gkv_far, gq, gq_far, media, mean, inv, latents)
    inputs += (grad_middle.reshape(images, latent_rows, width),)
    weights = (query_weight, key_weight, value_weight, weights_far, vectors[0], vectors[2])
    part = images // 2
    early = inputs_back(0, part, (), after(gkv, down_leave), *inputs, weights + (feed_vec,))
    done = down.advance(small.advance(early[2], feed_far))
    up_leave, up_keep = up_side(
        member, place, fl, cl, slope, down_weight, after(grad_pre, done), devices
    )

    hops = [near_bit * (at & 1) + far_bit * (at >> 1) for at in range(GROUP)]

    def pieces(mixed):
        return [mixed[0]] + [links.send(mixed[at], hops[at], hops[at]) for at in range(1, GROUP)]

    done = up_leave
    while down.left > 1:
        done = down.advance(done)
    mixed = down.advance(done)
    up = Halving(links, after(up_leave, mixed), up_keep, wide_orders)
    down_pieces = pieces(mixed)
    grad_media, grad_latents, vec = inputs_back(
        part, images - part, early[:2], after(gkv, mixed), *inputs, weights + (early[2],)
    )
    down_pieces = list(lax.optimization_barrier(tuple(down_pieces) + (vec,)))
    done = vec = down_pieces.pop()
    while up.left > 1:
        done = up.advance(done)
    vec = Total(links, after(vec, done), [group[1], group[0]] + wide_orders[0])
    done = small.advance(vec.array)
    done = result = (after(middle, done) + (feed_out + feed_far)).astype(HALF)
    done = vec.advance(done)
    mixed = up.advance(done)
    up_pieces = pieces(mixed)
    done = vec.advance(mixed, up_pieces[1])
    while small.left > 1:
        done = small.advance(done)
    down_pieces[0] = after(down_pieces[0], done)
    done = grad_down = place_pieces(member, down_pieces)
    while vec.order:
        done = vec.advance(done)
    vec = vec.advance(done, up_pieces[2], up_pieces[3])
    vec = lax.dynamic_slice_in_dim(vec, links.row * share, share, 1)
    up_pieces[0] = after(up_pieces[0], vec)
    grad_up = place_pieces(member, up_pieces)
    small = small.advance(grad_up)[0]
    return (
        result.reshape(latents.shape),
        grad_media,
        grad_latents,
        small[:, 2 * inner : 3 * inner],
        small[:, :inner],
        small[:, inner : 2 * inner],
        small[:, 3 * inner :].T,
        grad_up,
        grad_down.T,
    ) + tuple(vec[at] for at in range(6))


def solution(mesh):
    devices = mesh.shape["dp"]
    images = P("dp", None, None)
    columns = P(None, "tensor")
    lines = P("tensor", None)

    def body(*args):
        return local(*args, devices=devices)

    return jax.shard_map(
        body,
        mesh=mesh,
        in_specs=(images, P("dp"), images, images)
        + (columns, columns, columns, lines, columns, lines)
        + (P(),) * 6,
        out_specs=(images,) * 3
        + (P("dp", "tensor"),) * 3
        + (P("tensor", "dp"), P("dp", "tensor"), P("tensor", "dp"))
        + (P("dp"),) * 6,
        check_vma=False,
    )
```
